128 devices in a mesh: grp: 4 (over x), dev: 32 (over z, y, core).
Axes of the slice: x: 4, y: 4, z: 4, core: 2. Of those that a mesh axis runs over, the one named last changes fastest.
Arguments:
- cache_k: bfloat16 [64, 8, 1024, 128], P('grp', None, 'dev')
- cache_v: bfloat16 [64, 8, 1024, 128], P('grp', None, 'dev'), may hold values from -6 to 6
- source: int32 [64], replicated, may hold values from 0 to 63, as said below
- lengths: int32 [64], P('grp'), may hold values from 1 to 1023
- query: bfloat16 [64, 6144], P('grp')
- new_key: bfloat16 [64, 8, 128], P('grp'), may hold values from -6 to 6
- new_value: bfloat16 [64, 8, 128], P('grp'), may hold values from -6 to 6
- resid: bfloat16 [64, 6144], P('grp', 'dev'), may hold values from -6 to 6
- out_weight: bfloat16 [6144, 6144], P('dev'), may hold values from -0.078125 to 0.078125
- norm_gain: bfloat16 [6144], replicated, may hold values from 0.099609375 to 1.8984375
- w_gate: bfloat16 [6144, 65536], P(None, ('grp', 'dev')), may hold values from -0.078125 to 0.078125
- w_up: bfloat16 [6144, 65536], P(None, ('grp', 'dev')), may hold values from -0.078125 to 0.078125
- w_down: bfloat16 [65536, 6144], P(('grp', 'dev')), may hold values from -0.0625 to 0.0625
- expert_ids: int32 [64, 2], P('grp'), may hold values from 0 to 7, all different within a row; in each aligned block of 16 rows (0 to 15, 16 to 31, ...) at most 8 rows name the same one
- gate_codes: int32 [64, 2], P('grp'), may hold values from 1 to 1023
Outputs:
- new_cache_k: bfloat16 [64, 8, 1024, 128], P('grp', None, 'dev')
- new_cache_v: bfloat16 [64, 8, 1024, 128], P('grp', None, 'dev')
- layer_out: bfloat16 [64, 6144], P('grp', 'dev')
The draws below stay inside these ranges and needn't reach their ends.
Inputs may be any that keep to these rules, and one draw needn't show every extreme that they name: source is a permutation of the 64 slots; each group of 16 slots sends exactly 2 of its requests to each other group and receives exactly 2 from each other group into the slots it vacated; every other slot keeps its own request. `expert_ids`: in the 16 rows of each group no expert is named more than 8 times.
All inputs are finite; a program needn't handle non-finite values.
Results may differ from the reference program's by a relative error of at most 0.012.
Values may be sent and summed in bfloat16 or wider, within the bound.
No kernel may reach another device: no remote copies, remote signals or barrier semaphores. Data moves between devices by JAX's collectives and lax.ppermute only.
A program may use at most 128 MiB of HBM per device.

```python
import math
import jax
import jax.numpy as jnp
import numpy as np
from jax import lax

D = 6144
HEADS = 48
KV_HEADS = 8
HEAD_DIM = 128
EXPERTS = 8
FF = 8192
TOP = 2
REQ_G = 16
GQ = 6
LEN = 1024
REQS = 64
MOVE = 2
CAP = 8


def align_pattern(key):
    base = jax.random.fold_in(key, 7)
    magnitude = jax.random.uniform(jax.random.fold_in(base, 1), (KV_HEADS, HEAD_DIM), jnp.float32, 2.8, 3.0)
    flips = jax.random.bernoulli(jax.random.fold_in(base, 2), 0.5, (KV_HEADS, HEAD_DIM))
    return jnp.where(flips, magnitude, -magnitude)


def draw_query(key, part):
    shape = (REQS, HEADS * HEAD_DIM)
    values = jax.random.normal(jax.random.fold_in(key, 11), shape, jnp.float32)
    pattern = align_pattern(key)
    strength = jax.random.uniform(jax.random.fold_in(key, 13), (REQS,), jnp.float32, 1.5, 6.0)
    chosen = jax.random.uniform(jax.random.fold_in(key, 14), (REQS,), jnp.float32) < 0.3
    aligned = jnp.broadcast_to(pattern[None, :, None, :], (REQS, KV_HEADS, GQ, HEAD_DIM)) * strength[:, None, None, None]
    values = jnp.where(chosen[:, None], aligned.reshape(shape), values)
    return values.astype(jnp.bfloat16)


def draw_cache_k(key, part):
    shape = (REQS, KV_HEADS, LEN, HEAD_DIM)
    values = jax.random.normal(jax.random.fold_in(key, 17), shape, jnp.float32)
    pattern = align_pattern(key)
    positions = jnp.arange(LEN)[None, None, :, None]
    first = jnp.broadcast_to(pattern[None, :, None, :], shape)
    values = jnp.where(positions == 0, first, values)
    values = jnp.where(positions == 1, first * 0.99, values)
    return values.astype(jnp.bfloat16)


def draw_source(key, part):
    group_count = REQS // REQ_G
    leave_count = MOVE * (group_count - 1)
    groups = jnp.arange(group_count, dtype=jnp.int32)

    def shuffle_of(group):
        return jax.random.permutation(jax.random.fold_in(jax.random.fold_in(key, 22), group), REQ_G).astype(jnp.int32)
    shuffled = jax.vmap(shuffle_of)(groups)
    leave_range = jnp.arange(leave_count, dtype=jnp.int32)
    from_group = (groups[:, None] - 1 - leave_range[None, :] // MOVE) % group_count
    from_slot = shuffled[from_group, jnp.broadcast_to(leave_range[None, :], (group_count, leave_count))]
    stays = groups[:, None] * REQ_G + jnp.arange(REQ_G, dtype=jnp.int32)[None, :]
    target_rows = jnp.broadcast_to(groups[:, None], (group_count, leave_count))
    result = stays.at[target_rows, shuffled[:, :leave_count]].set(from_group * REQ_G + from_slot)
    return result.reshape(-1).astype(jnp.int32)


def set_ends(drawn, own_key, low, largest):
    dims = drawn.shape
    index_at = [jax.random.randint(jax.random.fold_in(own_key, axis), (), 0, dims[axis]) for axis in range(len(dims))]
    drawn = drawn.at[tuple(index_at)].set(low)
    longest = dims.index(max(dims))
    index_at[longest] = (index_at[longest] + 1) % dims[longest]
    return drawn.at[tuple(index_at)].set(largest)


def shard_levels(own_key, extent, shards, low, top_value):
    def one(dim, blocks):
        heights = jax.random.uniform(jax.random.fold_in(jax.random.fold_in(own_key, 6), dim), (blocks,), jnp.float32, low / len(shards), top_value / len(shards))
        return jnp.repeat(jnp.exp(heights), extent[dim] // blocks).reshape((-1,) + (1,) * (len(extent) - dim - 1))

    factor_of = one(*shards[0])
    for cut in shards[1:]:
        factor_of = factor_of * one(*cut)
    return factor_of


def shared_out(rng, own, number, rows, amount, top, reach, skew):
    ranking = jax.random.permutation(rng, amount)
    packed, usual = load_shares(amount, rows * top, reach, skew, True), load_shares(amount, rows * top, reach, skew, False)
    places = jnp.arange(amount)

    def named(sizes, offset_by):
        used = int((sizes > 0).sum())
        fixed = max(1, used // 4)
        shifted = fixed + (places - fixed + offset_by * (used - fixed)) % max(1, amount - fixed)
        return jnp.zeros((amount,), jnp.int32).at[ranking[jnp.where(places < fixed, places, shifted)]].set(jnp.asarray(sizes, jnp.int32))

    sizes = jnp.where(number % 4 == 0, named(packed, number // 4), named(usual, number - number // 4 - 1))
    mixed = jax.random.permutation(jax.random.fold_in(own, 3), amount)
    giver, sink = mixed[0:amount // 2 * 2:2], mixed[1:amount // 2 * 2:2]
    margin = jnp.minimum(sizes[giver] - 1, reach - sizes[sink]) // 2
    margin = jnp.where((giver == ranking[0]) | (sink == ranking[0]) | (sizes[sink] == 0), 0, jnp.maximum(margin, 0))
    shifted = jax.random.randint(jax.random.fold_in(own, 4), (amount // 2,), 0, 1 << 20) % (margin + 1)
    sizes = sizes.at[giver].add(-shifted).at[sink].add(shifted)
    members = jnp.searchsorted(jnp.cumsum(sizes), jnp.arange(rows * top), side="right").astype(jnp.int32)
    grid = members.reshape(top, rows).T
    grid = grid[jax.random.permutation(jax.random.fold_in(own, 1), rows)]
    offset_by = jax.random.randint(jax.random.fold_in(own, 2), (rows, 1), 0, top)
    return jnp.take_along_axis(grid, (jnp.arange(top)[None, :] + offset_by) % top, axis=1)


def load_shares(count, total, limit, lean, full):
    portions = [(1 << 20) // math.isqrt(grade ** lean) + 1 for grade in range(1, count + 1)]
    largest = limit if full else min(limit, max(-(-total // count), total * portions[0] // sum(portions)))
    least = 1 if total - largest >= count - 1 else 0
    holding, spare = [largest] + [least] * (count - 1), total - largest - least * (count - 1)
    while spare > 0:
        free = [i for i in range(1, count) if holding[i] < largest] or [i for i in range(1, count) if holding[i] < limit]
        whole, budget = sum([portions[i] for i in free]), spare
        for i in free:
            extra = min(limit - holding[i], max(1, budget * portions[i] // whole), spare)
            holding[i] = holding[i] + extra
            spare = spare - extra
    return np.array(holding)


def centred(rng, extent, scale, limit, split=(), held_as=jnp.bfloat16):
    values = scale * jax.random.normal(rng, extent, jnp.float32)
    if split:
        values = values * shard_levels(rng, extent, split, -0.22, 0.18)
    return jnp.clip(values, -limit, limit).astype(held_as)


def setup_inputs(seed: int = 0) -> dict:
    arg_keys = jax.random.split(jax.random.key(seed), 16)
    cache_k = draw_cache_k(jax.random.fold_in(arg_keys[15], 71), 0)
    cache_v = centred(arg_keys[1], (REQS, KV_HEADS, LEN, HEAD_DIM), 1.0, 6.0, ((0, 4), (2, 32)))
    source = draw_source(jax.random.fold_in(arg_keys[15], 71), 0)
    lengths = set_ends(jax.random.randint(arg_keys[3], (REQS,), 1, LEN), jax.random.fold_in(arg_keys[3], 1), 1, LEN - 1).astype(jnp.int32)
    query = draw_query(jax.random.fold_in(arg_keys[15], 71), 0)
    new_key = centred(arg_keys[5], (REQS, KV_HEADS, HEAD_DIM), 1.0, 6.0, ((0, 4),))
    new_value = centred(arg_keys[6], (REQS, KV_HEADS, HEAD_DIM), 1.0, 6.0, ((0, 4),))
    resid = centred(arg_keys[7], (REQS, D), 1.0, 6.0, ((0, 4), (1, 32)))
    out_weight = centred(arg_keys[8], (HEADS * HEAD_DIM, D), (HEADS * HEAD_DIM) ** -0.5, 0.078125, ((0, 32),))
    norm_gain = jnp.clip(1.0 + 0.18 * jax.random.normal(arg_keys[9], (D,), jnp.float32), 0.099609375, 1.8984375).astype(jnp.bfloat16)
    w_gate = centred(arg_keys[10], (D, EXPERTS * FF), D ** -0.5, 0.078125, ((1, 128),))
    w_up = centred(arg_keys[11], (D, EXPERTS * FF), D ** -0.5, 0.078125, ((1, 128),))
    w_down = centred(arg_keys[12], (EXPERTS * FF, D), FF ** -0.5, 0.0625, ((0, 128),))
    expert_ids_keys = jax.random.split(jax.random.fold_in(arg_keys[13], 1), REQS // REQ_G)
    expert_ids_turns = jax.random.permutation(jax.random.fold_in(arg_keys[13], 3), REQS // REQ_G)
    expert_ids = jax.vmap(lambda own, number: shared_out(jax.random.fold_in(arg_keys[13], 2), own, number, REQ_G, EXPERTS, TOP, CAP, 2))(expert_ids_keys, expert_ids_turns).reshape((REQS, TOP))
    gate_codes = set_ends(jax.random.randint(arg_keys[14], (REQS, TOP), 1, 1024), jax.random.fold_in(arg_keys[14], 1), 1, 1023).astype(jnp.int32)
    return dict(cache_k=cache_k, cache_v=cache_v, source=source, lengths=lengths, query=query, new_key=new_key, new_value=new_value, resid=resid, out_weight=out_weight, norm_gain=norm_gain, w_gate=w_gate, w_up=w_up, w_down=w_down, expert_ids=expert_ids, gate_codes=gate_codes)


def reference(cache_k, cache_v, source, lengths, query, new_key, new_value, resid, out_weight, norm_gain, w_gate, w_up, w_down, expert_ids, gate_codes):
    positions = jnp.arange(LEN, dtype=jnp.int32)
    hit = positions[None, :] == lengths[:, None]
    moved_k = jnp.take(cache_k, source, axis=0)
    moved_v = jnp.take(cache_v, source, axis=0)
    new_cache_k = jnp.where(hit[:, None, :, None], new_key[:, :, None, :], moved_k)
    new_cache_v = jnp.where(hit[:, None, :, None], new_value[:, :, None, :], moved_v)
    scale = 1.0 / HEAD_DIM ** 0.5

    def attend(items):
        keys, values, one_query, length = items
        grouped = one_query.astype(jnp.float32).reshape(KV_HEADS, GQ, HEAD_DIM)
        scores = jnp.einsum('kgh,kph->kgp', grouped, keys.astype(jnp.float32), precision=lax.Precision.HIGHEST) * scale
        valid = (positions <= length)[None, None, :]
        scores = jnp.where(valid, scores, jnp.float32(-1e+30))
        peak = lax.optimization_barrier(jnp.max(scores, axis=-1, keepdims=True))
        weights = jnp.where(valid, jnp.exp(scores - peak), jnp.float32(0.0))
        total = lax.optimization_barrier(jnp.sum(weights, axis=-1))
        context = jnp.einsum('kgp,kph->kgh', weights, values.astype(jnp.float32), precision=lax.Precision.HIGHEST)
        return (context / total[..., None]).reshape(HEADS * HEAD_DIM)
    attn = lax.map(attend, (new_cache_k, new_cache_v, query, lengths)).astype(jnp.bfloat16)
    mixed = resid.astype(jnp.float32) + jnp.dot(attn, out_weight, preferred_element_type=jnp.float32)
    mean_sq = lax.optimization_barrier(jnp.mean(mixed * mixed, axis=-1, keepdims=True))
    normed = (mixed * lax.rsqrt(mean_sq + 1e-05) * norm_gain.astype(jnp.float32)).astype(jnp.bfloat16)
    codes = gate_codes.astype(jnp.float32)
    gate_weight = codes / lax.optimization_barrier(jnp.sum(codes, axis=-1, keepdims=True))
    expert_range = jnp.arange(EXPERTS, dtype=jnp.int32)
    mixing = lax.optimization_barrier(jnp.sum(gate_weight[:, :, None] * (expert_ids[:, :, None] == expert_range[None, None, :]).astype(jnp.float32), axis=1))

    def run_expert(expert):
        start = (expert * FF).astype(jnp.int32)
        gate_cols = lax.dynamic_slice_in_dim(w_gate, start, FF, 1)
        up_cols = lax.dynamic_slice_in_dim(w_up, start, FF, 1)
        down_rows = lax.dynamic_slice_in_dim(w_down, start, FF, 0)
        gate_val = jnp.dot(normed, gate_cols, preferred_element_type=jnp.float32)
        up_val = jnp.dot(normed, up_cols, preferred_element_type=jnp.float32)
        hidden = (jax.nn.silu(gate_val) * up_val).astype(jnp.bfloat16)
        return jnp.dot(hidden, down_rows, preferred_element_type=jnp.float32)
    expert_out = lax.map(run_expert, expert_range)
    moe = lax.optimization_barrier(jnp.sum(mixing.T[:, :, None] * expert_out, axis=0))
    layer_out = (mixed + moe).astype(jnp.bfloat16)
    return (new_cache_k, new_cache_v, layer_out)
```

```python
import functools

import jax
import jax.numpy as jnp
from jax import lax
from jax.experimental import pallas as pl
from jax.experimental.pallas import tpu as pltpu
from jax.sharding import PartitionSpec as P

EXPERTS = 8
MOVE = 2
CAP = 8
LANES = 128
HALF = 64
F32 = jnp.float32
BF16 = jnp.bfloat16
VMEM = pl.BlockSpec(memory_space=pltpu.VMEM)
SMEM = pl.BlockSpec(memory_space=pltpu.SMEM)
ANY = pl.BlockSpec(memory_space=pl.ANY)


def pieces(value, count):
    terms = []
    for _ in range(count):
        term = value.astype(BF16).astype(F32)
        terms.append(term)
        value = value - term
    return terms


def iota(shape, dim):
    return lax.broadcasted_iota(jnp.int32, shape, dim)


def pack_kernel(groups, per, src, cache_k, cache_v, out, sem):
    me = lax.axis_index("grp")
    copies = []
    for dest in range(groups):
        count = jnp.int32(0)
        picks = [jnp.int32(0)] * MOVE
        for slot in range(per):
            old = src[dest * per + slot]
            mine = (old // per == me) & (me != dest)
            for rank in range(MOVE):
                picks[rank] = jnp.where(mine & (count == rank), old % per, picks[rank])
            count = count + mine.astype(jnp.int32)
        for rank in range(MOVE):
            for which, cache in ((0, cache_k), (1, cache_v)):
                copy = pltpu.make_async_copy(
                    cache.at[picks[rank]], out.at[dest, which, rank], sem.at[dest, which, rank]
                )
                copy.start()
                copies.append(copy)
    for copy in copies:
        copy.wait()


def attend_kernel(
    groups, per, src, length, cache_k, cache_v, recv, query, new_key, new_value,
    out_k, out_v, ctx, kbuf, vbuf, in_sem, out_sem,
):
    me = lax.axis_index("grp")
    dev = lax.axis_index("dev")
    heads_kv, block = kbuf.shape[1], kbuf.shape[2]
    share = query.shape[0] // heads_kv
    base = dev * block
    counts = [jnp.int32(0)] * groups
    for slot in range(per):
        old = src[me * per + slot]
        owner = old // per
        stays = owner == me
        rank = jnp.int32(0)
        for g in range(groups):
            here = owner == g
            rank = jnp.where(here, counts[g], rank)
            counts[g] = counts[g] + here.astype(jnp.int32)
        rank = jnp.minimum(rank, MOVE - 1)

        @pl.when(stays)
        def _():
            pltpu.make_async_copy(cache_k.at[old % per], kbuf.at[slot], in_sem.at[0, slot]).start()
            pltpu.make_async_copy(cache_v.at[old % per], vbuf.at[slot], in_sem.at[1, slot]).start()

        @pl.when(jnp.logical_not(stays))
        def _():
            pltpu.make_async_copy(recv.at[owner, 0, rank], kbuf.at[slot], in_sem.at[0, slot]).start()
            pltpu.make_async_copy(recv.at[owner, 1, rank], vbuf.at[slot], in_sem.at[1, slot]).start()

    col = iota((per, per * block), 1)
    row = iota((per, per * block), 0)
    limit = jnp.full((per, per * block), -1, jnp.int32)
    for slot in range(per):
        limit = jnp.where(row == slot, length[slot] - base, limit)
    valid = (col // block == row) & (col % block <= limit)

    outs = []
    for slot in range(per):
        pltpu.make_async_copy(cache_k.at[0], kbuf.at[slot], in_sem.at[0, slot]).wait()
        pltpu.make_async_copy(cache_v.at[0], vbuf.at[slot], in_sem.at[1, slot]).wait()
        spot = length[slot] - base

        @pl.when((spot >= 0) & (spot < block))
        def _():
            hit = iota((heads_kv, block, LANES), 1) == spot
            kbuf[slot] = jnp.where(hit, new_key[slot][:, None, :], kbuf[slot])
            vbuf[slot] = jnp.where(hit, new_value[slot][:, None, :], vbuf[slot])

        for which, buf, out in ((0, kbuf, out_k), (1, vbuf, out_v)):
            copy = pltpu.make_async_copy(buf.at[slot], out.at[slot], out_sem.at[which, slot])
            copy.start()
            outs.append(copy)

    lane = iota((1, 1, LANES), 2)
    scale = LANES**-0.5
    tiles, stats = [], []
    for kv in range(heads_kv):
        keys = kbuf[:, kv].reshape(per * block, LANES)
        values = vbuf[:, kv].reshape(per * block, LANES)
        rows = query[kv * share : (kv + 1) * share].reshape(share * per, LANES)
        scores = lax.dot_general(
            rows, keys, (((1,), (1,)), ((), ())), preferred_element_type=F32
        ).reshape(share, per, per * block) * scale
        scores = jnp.where(valid[None], scores, F32(-1e30))
        peak = jnp.max(scores, axis=-1, keepdims=True)
        weights = jnp.where(valid[None], jnp.exp(scores - peak), F32(0.0)).astype(BF16)
        total = jnp.sum(weights.astype(F32), axis=-1, keepdims=True)
        context = jnp.dot(
            weights.reshape(share * per, per * block), values, preferred_element_type=F32
        ).reshape(share, per, LANES)
        terms = pieces(peak, 3) + pieces(total, 2)
        stat = jnp.zeros((share, per, LANES), F32)
        for at, term in enumerate(terms):
            stat = jnp.where(lane % 8 == at, term, stat)
        for h in range(share):
            tiles.append(context[h])
            stats.append(stat[h])
    lane = iota((per, LANES), 1)
    first = (lane // 8) % 2 == 0
    low = lane < HALF
    for m in range(len(tiles) // 3):
        a, b, c = tiles[3 * m : 3 * m + 3]
        sa, sb, sc = stats[3 * m : 3 * m + 3]
        ctx[2 * m, 0] = a.astype(BF16)
        ctx[2 * m, 1] = jnp.where(low, b, jnp.where(first, sa, sb)).astype(BF16)
        ctx[2 * m + 1, 0] = jnp.where(low, jnp.where(first, sb, sc), b).astype(BF16)
        ctx[2 * m + 1, 1] = c.astype(BF16)
    for copy in outs:
        copy.wait()


def project_kernel(recv, weight, out):
    even = lax.axis_index("dev") % 2 == 0
    per = recv.shape[2]
    stat = jnp.where(even, recv[:, 1, :, HALF : HALF + 16], recv[:, 0, :, 0:16]).astype(F32)
    parts = []
    for k in range(2):
        at = 8 * k
        peak = stat[..., at : at + 1] + stat[..., at + 1 : at + 2] + stat[..., at + 2 : at + 3]
        total = stat[..., at + 3 : at + 4] + stat[..., at + 4 : at + 5]
        top = jnp.max(peak, axis=0, keepdims=True)
        factor = jnp.exp(peak - top)
        whole = jnp.sum(factor * total, axis=0)
        parts.append(jnp.sum(factor * recv[:, k].astype(F32), axis=0) / whole)
    both = jnp.concatenate(parts, axis=1)
    rows = weight.shape[0]
    attn = jnp.where(even, both[:, :rows], both[:, 2 * LANES - rows :]).astype(BF16)
    for m in range(out.shape[0] // 2):
        part = jnp.dot(
            attn, weight[:, 3 * LANES * m : 3 * LANES * (m + 1)], preferred_element_type=F32
        ).astype(BF16)
        t0, t1, t2 = (part[:, LANES * j : LANES * (j + 1)] for j in range(3))
        out[2 * m, 0] = t0
        out[2 * m, 1] = t1
        out[2 * m + 1, 0] = t1
        out[2 * m + 1, 1] = t2


def tiles_of(even, wide):
    rows = wide.shape[0]
    zero = jnp.zeros((rows, HALF), wide.dtype)
    left = jnp.concatenate([wide, zero], axis=1)
    right = jnp.concatenate([zero, wide], axis=1)
    both = jnp.where(even, left, right)
    return both[:, :LANES], both[:, LANES:]


def dispatch_kernel(recv, resid, gain, qrow, mixed, out):
    dev = lax.axis_index("dev")
    even = dev % 2 == 0
    per = recv.shape[2]
    lane = iota((per, LANES), 1)
    spare = (even & (lane >= HALF), jnp.logical_not(even) & (lane < HALF))
    spare = (spare[1], spare[0])
    start = tiles_of(even, resid[...].astype(F32))
    square = jnp.zeros((per, 1), F32)
    wides = []
    for k in range(2):
        part = start[k] + jnp.sum(recv[:, k].astype(F32), axis=0)
        part = jnp.where(spare[k], F32(0.0), part)
        mixed[k] = part
        square = square + jnp.sum(part * part, axis=1, keepdims=True)
        at = 3 * (dev // 2) + dev % 2 + k
        own = jnp.where(iota(gain.shape, 0) == at, gain[...].astype(F32), F32(0.0))
        wides.append(part * jnp.sum(own, axis=0, keepdims=True))
    stat = jnp.zeros((per, LANES), F32)
    for at, term in enumerate(pieces(square, 3)):
        stat = jnp.where(lane % 8 == at, term, stat)
    rows = jnp.concatenate(
        [jnp.where(spare[k], stat, wides[k]).astype(BF16) for k in range(2)], axis=0
    )
    count = EXPERTS * 2 * CAP
    where = iota((count, 2 * per), 0)
    from_ = iota((count, 2 * per), 1)
    slot = (where // (2 * CAP)) * CAP + where % CAP
    named = (slot == qrow[0:1, :]) | (slot == qrow[1:2, :])
    pick = (named & ((where // CAP) % 2 == from_ // per)).astype(F32).astype(BF16)
    sent = jnp.dot(pick, rows, preferred_element_type=F32).astype(BF16)
    split = out.shape[0] // EXPERTS
    for e in range(EXPERTS):
        block = sent[2 * CAP * e : 2 * CAP * (e + 1)]
        for s in range(split):
            out[e * split + s] = block


def expert_kernel(groups, recv, w_gate, w_up, w_down, out, xbuf, wg, wu, wd, sem):
    width = xbuf.shape[1]
    chunks = wg.shape[0]
    depth = wg.shape[1]
    copies = []
    for j in range(chunks):
        pair = []
        for which, (src, dst) in enumerate(((w_gate, wg), (w_up, wu))):
            copy = pltpu.make_async_copy(
                src.at[pl.ds(j * depth, depth), :], dst.at[j], sem.at[which, j]
            )
            copy.start()
            pair.append(copy)
        copies.append(pair)
    down_chunks = wd.shape[0]
    span = wd.shape[2]
    downs = []
    for j in range(down_chunks):
        copy = pltpu.make_async_copy(
            w_down.at[:, pl.ds(j * span, span)], wd.at[j], sem.at[2, j]
        )
        copy.start()
        downs.append(copy)
    devs = recv.shape[0] // groups
    lane = iota((CAP, LANES), 1)
    low = lane < HALF
    rows_square = []
    for g in range(groups):
        acc = jnp.zeros((CAP, LANES), F32)
        for m in range(devs // 2):
            e, o = recv[g * devs + 2 * m], recv[g * devs + 2 * m + 1]
            middle_e, middle_o = e[CAP:].astype(F32), o[:CAP].astype(F32)
            acc = acc + jnp.where(low, middle_o, middle_e)
            at = slice(CAP * g, CAP * (g + 1))
            xbuf[at, 3 * LANES * m : 3 * LANES * m + LANES] = e[:CAP]
            xbuf[at, 3 * LANES * m + LANES : 3 * LANES * m + 2 * LANES] = jnp.where(
                low, middle_e, middle_o
            ).astype(BF16)
            xbuf[at, 3 * LANES * m + 2 * LANES : 3 * LANES * (m + 1)] = o[CAP:]
        both = acc[:, :8] + acc[:, HALF : HALF + 8]
        rows_square.append(both[:, 0:1] + both[:, 1:2] + both[:, 2:3])
    square = jnp.concatenate(rows_square, axis=0)
    scale = lax.rsqrt(square / width + 1e-05)
    gate = jnp.zeros((groups * CAP, wg.shape[2]), F32)
    up = jnp.zeros((groups * CAP, wu.shape[2]), F32)
    for j in range(chunks):
        for copy in copies[j]:
            copy.wait()
        x = xbuf[:, depth * j : depth * (j + 1)]
        gate = gate + jnp.dot(x, wg[j], preferred_element_type=F32)
        up = up + jnp.dot(x, wu[j], preferred_element_type=F32)
    gate, up = gate * scale, up * scale
    hidden = (gate / (1.0 + jnp.exp(-gate)) * up).astype(BF16)
    per_chunk = span // (3 * LANES)
    for j in range(down_chunks):
        downs[j].wait()
        part = jnp.dot(hidden, wd[j], preferred_element_type=F32)
        for i in range(per_chunk):
            m = j * per_chunk + i
            t = [
                part[:, 3 * LANES * i + LANES * k : 3 * LANES * i + LANES * (k + 1)]
                for k in range(3)
            ]
            for g in range(groups):
                at = slice(CAP * g, CAP * (g + 1))
                out[g * devs + 2 * m] = jnp.concatenate([t[0][at], t[1][at]], axis=0).astype(BF16)
                out[g * devs + 2 * m + 1] = jnp.concatenate([t[1][at], t[2][at]], axis=0).astype(
                    BF16
                )


def final_kernel(recv, mixed, qcol, share, out):
    even = lax.axis_index("dev") % 2 == 0
    split = recv.shape[0] // EXPERTS
    per = mixed.shape[1]
    sums = [
        jnp.sum(recv[e * split : (e + 1) * split].astype(F32), axis=0) for e in range(EXPERTS)
    ]
    slot = iota((per, EXPERTS * CAP), 1)
    weight = jnp.where(slot == qcol[:, 0:1], share[:, 0:1], F32(0.0)) + jnp.where(
        slot == qcol[:, 1:2], share[:, 1:2], F32(0.0)
    )
    done = []
    for k in range(2):
        expert = jnp.concatenate([s[CAP * k : CAP * (k + 1)] for s in sums], axis=0)
        moe = jnp.dot(
            weight, expert, preferred_element_type=F32, precision=lax.Precision.HIGHEST
        )
        done.append(mixed[k] + moe)
    both = jnp.concatenate(done, axis=1)
    width = out.shape[1]
    out[...] = jnp.where(even, both[:, :width], both[:, 2 * LANES - width :]).astype(BF16)


def params(mib):
    return pltpu.CompilerParams(vmem_limit_bytes=mib << 20)


def on_device(
    cache_k,
    cache_v,
    source,
    lengths,
    query,
    new_key,
    new_value,
    resid,
    out_weight,
    norm_gain,
    w_gate,
    w_up,
    w_down,
    expert_ids,
    gate_codes,
):
    groups = lax.axis_size("grp")
    devs = lax.axis_size("dev")
    per, kv_heads, block, head_dim = cache_k.shape
    heads = query.shape[1] // head_dim
    width = query.shape[1]
    hidden = w_gate.shape[1]
    sds = jax.ShapeDtypeStruct
    move_shape = (groups, 2, MOVE, kv_heads, block, head_dim)

    sent = pl.pallas_call(
        functools.partial(pack_kernel, groups, per),
        name="pack",
        out_shape=sds(move_shape, BF16),
        in_specs=[SMEM, ANY, ANY],
        out_specs=VMEM,
        scratch_shapes=[pltpu.SemaphoreType.DMA((groups, 2, MOVE))],
        compiler_params=params(8),
    )(source, cache_k, cache_v)
    moved = lax.all_to_all(sent, "grp", split_axis=0, concat_axis=0, tiled=True)

    flat = expert_ids.reshape(-1)
    order = jnp.arange(flat.shape[0], dtype=jnp.int32)
    same = (flat[:, None] == flat[None, :]) & (order[None, :] < order[:, None])
    qflat = flat * CAP + jnp.sum(same.astype(jnp.int32), axis=1)
    qcol = qflat.reshape(per, 2)
    qrow = jnp.concatenate([qcol.T, qcol.T], axis=1)
    codes = gate_codes.astype(F32)
    share = codes / jnp.sum(codes, axis=-1, keepdims=True)
    by_head = query.reshape(per, heads, head_dim).transpose(1, 0, 2)

    new_k, new_v, ctx = pl.pallas_call(
        functools.partial(attend_kernel, groups, per),
        name="attend",
        out_shape=(
            sds(cache_k.shape, BF16),
            sds(cache_v.shape, BF16),
            sds((devs, 2, per, LANES), BF16),
        ),
        in_specs=[SMEM, SMEM, ANY, ANY, ANY, VMEM, VMEM, VMEM],
        out_specs=(ANY, ANY, VMEM),
        scratch_shapes=[
            pltpu.VMEM(cache_k.shape, BF16),
            pltpu.VMEM(cache_v.shape, BF16),
            pltpu.SemaphoreType.DMA((2, per)),
            pltpu.SemaphoreType.DMA((2, per)),
        ],
        compiler_params=params(16),
    )(source, lengths, cache_k, cache_v, moved, by_head, new_key, new_value)
    ctx = lax.all_to_all(ctx, "dev", split_axis=0, concat_axis=0, tiled=True)

    partial_rows = pl.pallas_call(
        project_kernel,
        name="project",
        out_shape=sds((devs, 2, per, LANES), BF16),
        in_specs=[VMEM, VMEM],
        out_specs=VMEM,
        compiler_params=params(12),
    )(ctx, out_weight)
    partial_rows = lax.all_to_all(partial_rows, "dev", split_axis=0, concat_axis=0, tiled=True)

    mixed, rows = pl.pallas_call(
        dispatch_kernel,
        name="dispatch",
        out_shape=(
            sds((2, per, LANES), F32),
            sds((groups * devs, 2 * CAP, LANES), BF16),
        ),
        in_specs=[VMEM] * 4,
        out_specs=(VMEM, VMEM),
        compiler_params=params(8),
    )(partial_rows, resid, norm_gain.reshape(-1, LANES), qrow)
    rows = lax.all_to_all(rows, ("grp", "dev"), split_axis=0, concat_axis=0, tiled=True)

    chunks, down_chunks = 8, 4
    partial_out = pl.pallas_call(
        functools.partial(expert_kernel, groups),
        name="expert",
        out_shape=sds((groups * devs, 2 * CAP, LANES), BF16),
        in_specs=[VMEM, ANY, ANY, ANY],
        out_specs=VMEM,
        scratch_shapes=[
            pltpu.VMEM((groups * CAP, width), BF16),
            pltpu.VMEM((chunks, width // chunks, hidden), BF16),
            pltpu.VMEM((chunks, width // chunks, hidden), BF16),
            pltpu.VMEM((down_chunks, hidden, width // down_chunks), BF16),
            pltpu.SemaphoreType.DMA((3, chunks)),
        ],
        compiler_params=params(32),
    )(rows, w_gate, w_up, w_down)
    partial_out = lax.all_to_all(
        partial_out, ("grp", "dev"), split_axis=0, concat_axis=0, tiled=True
    )

    layer_out = pl.pallas_call(
        final_kernel,
        name="final",
        out_shape=sds(resid.shape, BF16),
        in_specs=[VMEM] * 4,
        out_specs=VMEM,
        compiler_params=params(8),
    )(partial_out, mixed, qcol, share)
    return (new_k, new_v, layer_out)


def solution(mesh):
    in_specs = (
        P("grp", None, "dev", None),
        P("grp", None, "dev", None),
        P(),
        P("grp"),
        P("grp", None),
        P("grp", None, None),
        P("grp", None, None),
        P("grp", "dev"),
        P("dev", None),
        P(),
        P(None, ("grp", "dev")),
        P(None, ("grp", "dev")),
        P(("grp", "dev"), None),
        P("grp", None),
        P("grp", None),
    )
    out_specs = (P("grp", None, "dev", None), P("grp", None, "dev", None), P("grp", "dev"))
    return jax.shard_map(
        on_device, mesh=mesh, in_specs=in_specs, out_specs=out_specs, check_vma=False
    )
```

```python
import functools

import jax
import jax.numpy as jnp
from jax import lax
from jax.experimental import pallas as pl
from jax.experimental.pallas import tpu as pltpu
from jax.sharding import PartitionSpec as P

EXPERTS = 8
MOVE = 2
CAP = 8
LANES = 128
HALF = 64
F32 = jnp.float32
BF16 = jnp.bfloat16
VMEM = pl.BlockSpec(memory_space=pltpu.VMEM)
SMEM = pl.BlockSpec(memory_space=pltpu.SMEM)
HBM = pl.BlockSpec(memory_space=pltpu.HBM)


def pieces(value, count):
    terms = []
    for _ in range(count):
        term = value.astype(BF16).astype(F32)
        terms.append(term)
        value = value - term
    return terms


def iota(shape, dim):
    return lax.broadcasted_iota(jnp.int32, shape, dim)


def places(value, size):
    bits = size.bit_length() - 1
    assert size == 1 << bits
    return value >> bits, value & (size - 1)


def pack_kernel(groups, per, source, cache_k, cache_v, out, src, buf, src_sem, in_sem, out_sem):
    pltpu.make_async_copy(source, src, src_sem).start()
    me = lax.axis_index("grp")
    pltpu.make_async_copy(source, src, src_sem).wait()
    loads, stores = [], []
    for dest in range(groups):
        count = jnp.int32(0)
        picks = [jnp.int32(0)] * MOVE
        for slot in range(per):
            owner, old = places(src[dest * per + slot], per)
            mine = (owner == me) & (me != dest)
            for rank in range(MOVE):
                picks[rank] = jnp.where(mine & (count == rank), old, picks[rank])
            count = count + mine.astype(jnp.int32)
        for rank in range(MOVE):
            for which, cache in ((0, cache_k), (1, cache_v)):
                copy = pltpu.make_async_copy(
                    cache.at[picks[rank]], buf.at[dest, which, rank], in_sem.at[dest, which, rank]
                )
                copy.start()
                loads.append((copy, dest, which, rank))
    for load, dest, which, rank in loads:
        load.wait()
        copy = pltpu.make_async_copy(
            buf.at[dest, which, rank], out.at[dest, which, rank], out_sem.at[dest, which, rank]
        )
        copy.start()
        stores.append(copy)
    for copy in stores:
        copy.wait()


def column(values):
    rows = iota((len(values), 1), 0)
    result = jnp.zeros((len(values), 1), jnp.int32)
    for at, value in enumerate(values):
        result = jnp.where(rows == at, value, result)
    return result


def stay_kernel(
    groups, per, source, lengths, cache_k, cache_v, query, new_key, new_value, resid, gain,
    spare_valid, peaks, totals, contexts, start, gains, kbuf, vbuf, src, length, sems,
):
    copies = [
        pltpu.make_async_copy(a, b, sems.at[j])
        for j, (a, b) in enumerate(
            ((source, src), (lengths, length), (cache_k, kbuf), (cache_v, vbuf))
        )
    ]
    for copy in copies:
        copy.start()
    me = lax.axis_index("grp")
    heads_kv, block = kbuf.shape[1], kbuf.shape[2]
    share = query.shape[0] // heads_kv
    base = lax.axis_index("dev") * block
    copies[0].wait()
    copies[1].wait()
    counts = [jnp.int32(0)] * groups
    spots, limits, arrivals = [], [], []
    for slot in range(per):
        owner = places(src[me * per + slot], per)[0]
        rank = jnp.int32(0)
        for g in range(groups):
            here = owner == g
            rank = jnp.where(here, counts[g], rank)
            counts[g] = counts[g] + here.astype(jnp.int32)
        spot = length[slot] - base
        spots.append(spot)
        limits.append(jnp.where(owner == me, spot, -1))
        arrivals.append(jnp.where(owner == me, -1, owner * MOVE + rank))
    spot, limit, arrival = column(spots), column(limits), column(arrivals)
    which, where = places(iota((per, per * block), 1), block)
    valid = (which == iota((per, per * block), 0)) & (where < limit)
    which, where = places(iota((per, groups * MOVE * block), 1), block)
    spare_valid[...] = ((which == arrival) & (where < spot)).astype(F32)
    fresh = (spot >= 0) & (spot < block)
    copies[2].wait()
    copies[3].wait()
    scale = LANES**-0.5
    for kv in range(heads_kv):
        keys = kbuf[:, kv].reshape(per * block, LANES)
        values = vbuf[:, kv].reshape(per * block, LANES)
        rows = query[kv * share : (kv + 1) * share]
        scores = lax.dot_general(
            rows.reshape(share * per, LANES), keys, (((1,), (1,)), ((), ())),
            preferred_element_type=F32,
        ).reshape(share, per, per * block) * scale
        scores = jnp.where(valid[None], scores, F32(-1e30))
        newest = jnp.sum(
            rows.astype(F32) * new_key[kv].astype(F32)[None], axis=-1, keepdims=True
        ) * scale
        newest = jnp.where(fresh[None], newest, F32(-1e30))
        peak = jnp.maximum(jnp.max(scores, axis=-1, keepdims=True), newest)
        weights = jnp.where(valid[None], jnp.exp(scores - peak), F32(0.0)).astype(BF16)
        added = jnp.where(fresh[None], jnp.exp(newest - peak), F32(0.0))
        total = jnp.sum(weights.astype(F32), axis=-1, keepdims=True) + added
        context = jnp.dot(
            weights.reshape(share * per, per * block), values, preferred_element_type=F32
        ).reshape(share, per, LANES) + added * new_value[kv].astype(F32)[None]
        at = slice(kv * share, (kv + 1) * share)
        peaks[at] = jnp.broadcast_to(peak, (share, per, LANES))
        totals[at] = jnp.broadcast_to(total, (share, per, LANES))
        contexts[at] = context
    dev = lax.axis_index("dev")
    even = dev % 2 == 0
    tiles = tiles_of(even, resid[...].astype(F32))
    lane = iota((1, LANES), 1)
    spare = (jnp.logical_not(even) & (lane < HALF), even & (lane >= HALF))
    for k in range(2):
        start[k] = tiles[k]
        at = 3 * (dev // 2) + dev % 2 + k
        own = jnp.where(iota(gain.shape, 0) == at, gain[...].astype(F32), F32(0.0))
        gains[k : k + 1] = jnp.where(spare[k], F32(0.0), jnp.sum(own, axis=0, keepdims=True))


def arrive_kernel(moved, query, spare_valid, peaks, totals, contexts, out, buf, sems):
    groups, _, _, heads_kv, block, _ = moved.shape
    share, per = query.shape[0] // heads_kv, query.shape[1]
    columns = groups * MOVE * block
    valid = spare_valid[...] > 0.5
    scale = LANES**-0.5
    ones = jnp.ones((columns, LANES), BF16)
    lane = iota((1, 1, LANES), 2)
    lane2 = iota((per, LANES), 1)
    first = ((lane2 >> 3) & 1) == 0
    low = lane2 < HALF
    copies = []
    for kv in range(heads_kv):
        keys = moved[:, 0, :, kv].reshape(columns, LANES)
        values = moved[:, 1, :, kv].reshape(columns, LANES)
        at = slice(kv * share, (kv + 1) * share)
        scores = lax.dot_general(
            query[at].reshape(share * per, LANES), keys, (((1,), (1,)), ((), ())),
            preferred_element_type=F32,
        ).reshape(share, per, columns) * scale
        scores = jnp.where(valid[None], scores, F32(-1e30))
        before = peaks[at]
        peak = jnp.maximum(before, jnp.max(scores, axis=-1, keepdims=True))
        whole = jnp.concatenate([peak] * (columns // LANES), axis=-1)
        weights = jnp.where(valid[None], jnp.exp(scores - whole), F32(0.0)).astype(BF16)
        keep = jnp.exp(before - peak)
        sums = jnp.dot(
            weights.reshape(share * per, columns),
            jnp.concatenate([values, ones], axis=1),
            preferred_element_type=F32,
        ).reshape(share, per, 2 * LANES)
        context = sums[..., :LANES] + keep * contexts[at]
        total = sums[..., LANES:] + keep * totals[at]
        stat = jnp.zeros((share, per, LANES), F32)
        for j, term in enumerate(pieces(peak, 3) + pieces(total, 2)):
            stat = jnp.where((lane & 7) == j, term, stat)
        for i in range(share // 3):
            m = kv * (share // 3) + i
            a, b, c = (context[3 * i + j] for j in range(3))
            sa, sb, sc = (stat[3 * i + j] for j in range(3))
            buf[2 * m, 0] = a.astype(BF16)
            buf[2 * m, 1] = jnp.where(low, b, jnp.where(first, sa, sb)).astype(BF16)
            buf[2 * m + 1, 0] = jnp.where(low, jnp.where(first, sb, sc), b).astype(BF16)
            buf[2 * m + 1, 1] = c.astype(BF16)
        part = pl.ds(2 * kv * (share // 3), 2 * (share // 3))
        copy = pltpu.make_async_copy(buf.at[part], out.at[part], sems.at[kv])
        copy.start()
        copies.append(copy)
    for copy in copies:
        copy.wait()


def store_kernel(
    groups, per, source, lengths, cache_k, cache_v, moved, new_key, new_value,
    out_k, out_v, kbuf, vbuf, src, length, small_sem, in_sem, out_sem,
):
    small = [
        pltpu.make_async_copy(source, src, small_sem.at[0]),
        pltpu.make_async_copy(lengths, length, small_sem.at[1]),
    ]
    for copy in small:
        copy.start()
    me = lax.axis_index("grp")
    heads_kv, block = kbuf.shape[1], kbuf.shape[2]
    base = lax.axis_index("dev") * block
    for copy in small:
        copy.wait()
    counts = [jnp.int32(0)] * groups
    for slot in range(per):
        owner = places(src[me * per + slot], per)[0]
        stays = owner == me
        rank = jnp.int32(0)
        for g in range(groups):
            here = owner == g
            rank = jnp.where(here, counts[g], rank)
            counts[g] = counts[g] + here.astype(jnp.int32)
        rank = jnp.minimum(rank, MOVE - 1)

        @pl.when(stays)
        def _():
            pltpu.make_async_copy(cache_k.at[slot], kbuf.at[slot], in_sem.at[0, slot]).start()
            pltpu.make_async_copy(cache_v.at[slot], vbuf.at[slot], in_sem.at[1, slot]).start()

        @pl.when(jnp.logical_not(stays))
        def _():
            pltpu.make_async_copy(moved.at[owner, 0, rank], kbuf.at[slot], in_sem.at[0, slot]).start()
            pltpu.make_async_copy(moved.at[owner, 1, rank], vbuf.at[slot], in_sem.at[1, slot]).start()

    outs = []
    for slot in range(per):
        pltpu.make_async_copy(cache_k.at[0], kbuf.at[slot], in_sem.at[0, slot]).wait()
        pltpu.make_async_copy(cache_v.at[0], vbuf.at[slot], in_sem.at[1, slot]).wait()
        spot = length[slot] - base

        @pl.when((spot >= 0) & (spot < block))
        def _():
            hit = iota((heads_kv, block, LANES), 1) == spot
            kbuf[slot] = jnp.where(hit, new_key[slot][:, None, :], kbuf[slot])
            vbuf[slot] = jnp.where(hit, new_value[slot][:, None, :], vbuf[slot])

        for which, buf, out in ((0, kbuf, out_k), (1, vbuf, out_v)):
            copy = pltpu.make_async_copy(buf.at[slot], out.at[slot], out_sem.at[which, slot])
            copy.start()
            outs.append(copy)
    for copy in outs:
        copy.wait()


def project_kernel(recv, weight, out, wbuf, buf, w_sems, sems):
    span = wbuf.shape[2]
    loads = []
    for j in range(wbuf.shape[0]):
        copy = pltpu.make_async_copy(
            weight.at[:, pl.ds(j * span, span)], wbuf.at[j], w_sems.at[j]
        )
        copy.start()
        loads.append(copy)
    even = lax.axis_index("dev") % 2 == 0
    per = recv.shape[2]
    peers = recv.shape[0]
    stat = jnp.where(even, recv[:, 1], recv[:, 0]).reshape(peers * per, LANES)
    kind, _ = places(iota((LANES, 4 * LANES), 1), LANES)
    term = iota((LANES, 4 * LANES), 0) - jnp.where(even, HALF, 0) - 8 * (kind >> 1)
    begin = 3 * (kind & 1)
    wanted = (term >= begin) & (term < 3 + 2 * (kind & 1))
    spread = jnp.dot(
        stat, wanted.astype(F32).astype(BF16), preferred_element_type=F32
    ).reshape(peers, per, 4 * LANES)
    parts = []
    for k in range(2):
        peak = spread[..., 2 * k * LANES : (2 * k + 1) * LANES]
        total = spread[..., (2 * k + 1) * LANES : (2 * k + 2) * LANES]
        factor = jnp.exp(peak - jnp.max(peak, axis=0, keepdims=True))
        whole = jnp.sum(factor * total, axis=0)
        parts.append(jnp.sum(factor * recv[:, k].astype(F32), axis=0) / whole)
    both = jnp.concatenate(parts, axis=1)
    rows = weight.shape[0]
    attn = jnp.where(even, both[:, :rows], both[:, 2 * LANES - rows :]).astype(BF16)
    copies = []
    for m in range(out.shape[0] // 2):
        j, at = divmod(3 * LANES * m, span)
        if at == 0:
            loads[j].wait()
        part = jnp.dot(
            attn, wbuf[j, :, at : at + 3 * LANES], preferred_element_type=F32
        ).astype(BF16)
        t0, t1, t2 = (part[:, LANES * j : LANES * (j + 1)] for j in range(3))
        buf[2 * m, 0] = t0
        buf[2 * m, 1] = t1
        buf[2 * m + 1, 0] = t1
        buf[2 * m + 1, 1] = t2
        part = pl.ds(2 * m, 2)
        copy = pltpu.make_async_copy(buf.at[part], out.at[part], sems.at[m])
        copy.start()
        copies.append(copy)
    for copy in copies:
        copy.wait()


def tiles_of(even, wide):
    rows = wide.shape[0]
    zero = jnp.zeros((rows, HALF), wide.dtype)
    left = jnp.concatenate([wide, zero], axis=1)
    right = jnp.concatenate([zero, wide], axis=1)
    both = jnp.where(even, left, right)
    return both[:, :LANES], both[:, LANES:]


def dispatch_kernel(recv, start, gains, qrow, mixed, out):
    even = lax.axis_index("dev") % 2 == 0
    per = recv.shape[2]
    lane = iota((per, LANES), 1)
    spare = (jnp.logical_not(even) & (lane < HALF), even & (lane >= HALF))
    square = jnp.zeros((per, 1), F32)
    wides = []
    for k in range(2):
        part = start[k] + jnp.sum(recv[:, k].astype(F32), axis=0)
        part = jnp.where(spare[k], F32(0.0), part)
        mixed[k] = part
        square = square + jnp.sum(part * part, axis=1, keepdims=True)
        wides.append(part * gains[k : k + 1])
    stat = jnp.zeros((per, LANES), F32)
    for at, term in enumerate(pieces(square, 3)):
        stat = jnp.where((lane & 7) == at, term, stat)
    rows = jnp.concatenate(
        [jnp.where(spare[k], stat, wides[k]).astype(BF16) for k in range(2)], axis=0
    )
    count = EXPERTS * 2 * CAP
    where = iota((count, 2 * per), 0)
    from_ = iota((count, 2 * per), 1)
    expert, _ = places(where, 2 * CAP)
    half, place = places(where, CAP)
    slot = expert * CAP + place
    named = (slot == qrow[0:1, :]) | (slot == qrow[1:2, :])
    pick = (named & ((half & 1) == places(from_, per)[0])).astype(F32).astype(BF16)
    sent = jnp.dot(pick, rows, preferred_element_type=F32).astype(BF16)
    split = out.shape[0] // EXPERTS
    for e in range(EXPERTS):
        block = sent[2 * CAP * e : 2 * CAP * (e + 1)]
        for s in range(split):
            out[e * split + s] = block


def expert_kernel(groups, recv, w_gate, w_up, w_down, out, xbuf, buf, wg, wu, wd, w_sems, sems):
    width = xbuf.shape[1]
    depth, span = wg.shape[1], wd.shape[2]
    firsts, seconds = [], []
    for j in range(wg.shape[0]):
        rows = pl.ds(j * depth, depth)
        pair = (
            pltpu.make_async_copy(w_gate.at[rows], wg.at[j], w_sems.at[0, j]),
            pltpu.make_async_copy(w_up.at[rows], wu.at[j], w_sems.at[1, j]),
        )
        for copy in pair:
            copy.start()
        firsts.append(pair)
    for j in range(wd.shape[0]):
        copy = pltpu.make_async_copy(
            w_down.at[:, pl.ds(j * span, span)], wd.at[j], w_sems.at[2, j]
        )
        copy.start()
        seconds.append(copy)
    devs = recv.shape[0] // groups
    lane = iota((CAP, LANES), 1)
    low = lane < HALF
    rows_square = []
    for g in range(groups):
        acc = jnp.zeros((CAP, LANES), F32)
        for m in range(devs // 2):
            e, o = recv[g * devs + 2 * m], recv[g * devs + 2 * m + 1]
            middle_e, middle_o = e[CAP:].astype(F32), o[:CAP].astype(F32)
            acc = acc + jnp.where(low, middle_o, middle_e)
            at = slice(CAP * g, CAP * (g + 1))
            xbuf[at, 3 * LANES * m : 3 * LANES * m + LANES] = e[:CAP]
            xbuf[at, 3 * LANES * m + LANES : 3 * LANES * m + 2 * LANES] = jnp.where(
                low, middle_e, middle_o
            ).astype(BF16)
            xbuf[at, 3 * LANES * m + 2 * LANES : 3 * LANES * (m + 1)] = o[CAP:]
        both = acc[:, :8] + acc[:, HALF : HALF + 8]
        rows_square.append(both[:, 0:1] + both[:, 1:2] + both[:, 2:3])
    square = jnp.concatenate(rows_square, axis=0)
    scale = lax.rsqrt(square / width + 1e-05)
    gate = jnp.zeros((groups * CAP, wg.shape[2]), F32)
    up = jnp.zeros((groups * CAP, wu.shape[2]), F32)
    for j, pair in enumerate(firsts):
        x = xbuf[:, depth * j : depth * (j + 1)]
        pair[0].wait()
        gate = gate + jnp.dot(x, wg[j], preferred_element_type=F32)
        pair[1].wait()
        up = up + jnp.dot(x, wu[j], preferred_element_type=F32)
    gate, up = gate * scale, up * scale
    hidden = (gate / (1.0 + jnp.exp(-gate)) * up).astype(BF16)
    copies = []
    for m in range(devs // 2):
        j, at = divmod(3 * LANES * m, span)
        if at == 0:
            seconds[j].wait()
        part = jnp.dot(
            hidden, wd[j, :, at : at + 3 * LANES], preferred_element_type=F32
        )
        t = [part[:, LANES * k : LANES * (k + 1)] for k in range(3)]
        for g in range(groups):
            at = slice(CAP * g, CAP * (g + 1))
            for i in range(2):
                buf[g, 2 * m + i] = jnp.concatenate([t[i][at], t[i + 1][at]], axis=0).astype(BF16)
            copy = pltpu.make_async_copy(
                buf.at[g, pl.ds(2 * m, 2)], out.at[pl.ds(g * devs + 2 * m, 2)], sems.at[g, m]
            )
            copy.start()
            copies.append(copy)
    for copy in copies:
        copy.wait()


def final_kernel(recv, mixed, qcol, share, out):
    even = lax.axis_index("dev") % 2 == 0
    split = recv.shape[0] // EXPERTS
    per = mixed.shape[1]
    sums = [
        jnp.sum(recv[e * split : (e + 1) * split].astype(F32), axis=0) for e in range(EXPERTS)
    ]
    slot = iota((per, EXPERTS * CAP), 1)
    weight = jnp.where(slot == qcol[:, 0:1], share[:, 0:1], F32(0.0)) + jnp.where(
        slot == qcol[:, 1:2], share[:, 1:2], F32(0.0)
    )
    done = []
    for k in range(2):
        expert = jnp.concatenate([s[CAP * k : CAP * (k + 1)] for s in sums], axis=0)
        moe = jnp.dot(
            weight, expert, preferred_element_type=F32, precision=lax.Precision.HIGHEST
        )
        done.append(mixed[k] + moe)
    both = jnp.concatenate(done, axis=1)
    width = out.shape[1]
    out[...] = jnp.where(even, both[:, :width], both[:, 2 * LANES - width :]).astype(BF16)


def params(free):
    return pltpu.CompilerParams(vmem_limit_bytes=67043328 - free)


def on_device(
    cache_k,
    cache_v,
    source,
    lengths,
    query,
    new_key,
    new_value,
    resid,
    out_weight,
    norm_gain,
    w_gate,
    w_up,
    w_down,
    expert_ids,
    gate_codes,
):
    groups = lax.axis_size("grp")
    devs = lax.axis_size("dev")
    per, kv_heads, block, head_dim = cache_k.shape
    heads = query.shape[1] // head_dim
    width = query.shape[1]
    hidden = w_gate.shape[1]
    sds = jax.ShapeDtypeStruct
    cache_k, cache_v, source, lengths, out_weight, w_gate, w_up, w_down = (
        pltpu.with_memory_space_constraint(a, pltpu.HBM)
        for a in (cache_k, cache_v, source, lengths, out_weight, w_gate, w_up, w_down)
    )
    move_shape = (groups, 2, MOVE, kv_heads, block, head_dim)

    sent = pl.pallas_call(
        functools.partial(pack_kernel, groups, per),
        name="pack",
        out_shape=sds(move_shape, BF16),
        in_specs=[HBM, HBM, HBM],
        out_specs=HBM,
        scratch_shapes=[
            pltpu.SMEM(source.shape, jnp.int32),
            pltpu.VMEM(move_shape, BF16),
            pltpu.SemaphoreType.DMA,
            pltpu.SemaphoreType.DMA((groups, 2, MOVE)),
            pltpu.SemaphoreType.DMA((groups, 2, MOVE)),
        ],
        compiler_params=params(56 << 20),
    )(source, cache_k, cache_v)
    moved = lax.all_to_all(sent, "grp", split_axis=0, concat_axis=0, tiled=True)

    flat = expert_ids.reshape(-1)
    order = jnp.arange(flat.shape[0], dtype=jnp.int32)
    same = (flat[:, None] == flat[None, :]) & (order[None, :] < order[:, None])
    qflat = flat * CAP + jnp.sum(same.astype(jnp.int32), axis=1)
    qcol = qflat.reshape(per, 2)
    qrow = jnp.concatenate([qcol.T, qcol.T], axis=1)
    codes = gate_codes.astype(F32)
    share = codes / jnp.sum(codes, axis=-1, keepdims=True)
    by_head = query.reshape(per, heads, head_dim).transpose(1, 0, 2)

    row_shape = sds((heads, per, LANES), F32)
    spare_valid, peaks, totals, contexts, start, gains = pl.pallas_call(
        functools.partial(stay_kernel, groups, per),
        name="stay",
        out_shape=(
            sds((per, groups * MOVE * block), F32),
            row_shape,
            row_shape,
            row_shape,
            sds((2, per, LANES), F32),
            sds((2, LANES), F32),
        ),
        in_specs=[HBM, HBM, HBM, HBM, VMEM, VMEM, VMEM, VMEM, VMEM],
        out_specs=(VMEM,) * 6,
        scratch_shapes=[
            pltpu.VMEM(cache_k.shape, BF16),
            pltpu.VMEM(cache_v.shape, BF16),
            pltpu.SMEM(source.shape, jnp.int32),
            pltpu.SMEM(lengths.shape, jnp.int32),
            pltpu.SemaphoreType.DMA((4,)),
        ],
        compiler_params=params(48 << 20),
        cost_estimate=pl.CostEstimate(flops=0, transcendentals=0, bytes_accessed=16 << 20),
    )(
        source, lengths, cache_k, cache_v, by_head,
        new_key.transpose(1, 0, 2), new_value.transpose(1, 0, 2), resid,
        norm_gain.reshape(-1, LANES),
    )

    ctx = pl.pallas_call(
        arrive_kernel,
        name="arrive",
        out_shape=sds((devs, 2, per, LANES), BF16),
        in_specs=[VMEM] * 6,
        out_specs=HBM,
        scratch_shapes=[
            pltpu.VMEM((devs, 2, per, LANES), BF16),
            pltpu.SemaphoreType.DMA((kv_heads,)),
        ],
        compiler_params=params(52 << 20),
    )(moved, by_head, spare_valid, peaks, totals, contexts)
    ctx = lax.all_to_all(ctx, "dev", split_axis=0, concat_axis=0, tiled=True)

    new_k, new_v = pl.pallas_call(
        functools.partial(store_kernel, groups, per),
        name="store",
        out_shape=(sds(cache_k.shape, BF16), sds(cache_v.shape, BF16)),
        in_specs=[HBM, HBM, HBM, HBM, pl.BlockSpec(memory_space=pl.ANY), VMEM, VMEM],
        out_specs=(HBM, HBM),
        scratch_shapes=[
            pltpu.VMEM(cache_k.shape, BF16),
            pltpu.VMEM(cache_v.shape, BF16),
            pltpu.SMEM(source.shape, jnp.int32),
            pltpu.SMEM(lengths.shape, jnp.int32),
            pltpu.SemaphoreType.DMA((2,)),
            pltpu.SemaphoreType.DMA((2, per)),
            pltpu.SemaphoreType.DMA((2, per)),
        ],
        compiler_params=params(52 << 20),
        cost_estimate=pl.CostEstimate(flops=0, transcendentals=0, bytes_accessed=8 << 20),
    )(source, lengths, cache_k, cache_v, moved, new_key, new_value)

    partial_rows = pl.pallas_call(
        project_kernel,
        name="project",
        out_shape=sds((devs, 2, per, LANES), BF16),
        in_specs=[VMEM, HBM],
        out_specs=HBM,
        scratch_shapes=[
            pltpu.VMEM((8, out_weight.shape[0], width // 8), BF16),
            pltpu.VMEM((devs, 2, per, LANES), BF16),
            pltpu.SemaphoreType.DMA((8,)),
            pltpu.SemaphoreType.DMA((devs // 2,)),
        ],
        compiler_params=params(52 << 20),
    )(ctx, out_weight)
    partial_rows = lax.all_to_all(partial_rows, "dev", split_axis=0, concat_axis=0, tiled=True)

    mixed, rows = pl.pallas_call(
        dispatch_kernel,
        name="dispatch",
        out_shape=(
            sds((2, per, LANES), F32),
            sds((groups * devs, 2 * CAP, LANES), BF16),
        ),
        in_specs=[VMEM] * 4,
        out_specs=(VMEM, VMEM),
        compiler_params=params(56 << 20),
    )(partial_rows, start, gains, qrow)
    rows = lax.all_to_all(rows, ("grp", "dev"), split_axis=0, concat_axis=0, tiled=True)

    chunks, down_chunks = 12, 8
    partial_out = pl.pallas_call(
        functools.partial(expert_kernel, groups),
        name="expert",
        out_shape=sds((groups * devs, 2 * CAP, LANES), BF16),
        in_specs=[VMEM, HBM, HBM, HBM],
        out_specs=HBM,
        scratch_shapes=[
            pltpu.VMEM((groups * CAP, width), BF16),
            pltpu.VMEM((groups, devs, 2 * CAP, LANES), BF16),
            pltpu.VMEM((chunks, width // chunks, hidden), BF16),
            pltpu.VMEM((chunks, width // chunks, hidden), BF16),
            pltpu.VMEM((down_chunks, hidden, width // down_chunks), BF16),
            pltpu.SemaphoreType.DMA((3, chunks)),
            pltpu.SemaphoreType.DMA((groups, devs // 2)),
        ],
        compiler_params=params(32 << 20),
    )(rows, w_gate, w_up, w_down)
    partial_out = lax.all_to_all(
        partial_out, ("grp", "dev"), split_axis=0, concat_axis=0, tiled=True
    )

    layer_out = pl.pallas_call(
        final_kernel,
        name="final",
        out_shape=sds(resid.shape, BF16),
        in_specs=[VMEM] * 4,
        out_specs=VMEM,
        compiler_params=params(56 << 20),
    )(partial_out, mixed, qcol, share)
    return (new_k, new_v, layer_out)


def solution(mesh):
    in_specs = (
        P("grp", None, "dev", None),
        P("grp", None, "dev", None),
        P(),
        P("grp"),
        P("grp", None),
        P("grp", None, None),
        P("grp", None, None),
        P("grp", "dev"),
        P("dev", None),
        P(),
        P(None, ("grp", "dev")),
        P(None, ("grp", "dev")),
        P(("grp", "dev"), None),
        P("grp", None),
        P("grp", None),
    )
    out_specs = (P("grp", None, "dev", None), P("grp", None, "dev", None), P("grp", "dev"))
    return jax.shard_map(
        on_device, mesh=mesh, in_specs=in_specs, out_specs=out_specs, check_vma=False
    )
```

```python
import functools

import jax
import jax.numpy as jnp
from jax import lax
from jax.experimental import pallas as pl
from jax.experimental.pallas import tpu as pltpu
from jax.sharding import PartitionSpec as P

EXPERTS = 8
MOVE = 2
CAP = 8
LANES = 128
HALF = 64
F32 = jnp.float32
BF16 = jnp.bfloat16
VMEM = pl.BlockSpec(memory_space=pltpu.VMEM)
SMEM = pl.BlockSpec(memory_space=pltpu.SMEM)
HBM = pl.BlockSpec(memory_space=pltpu.HBM)


def pieces(value, count):
    terms = []
    for _ in range(count):
        term = value.astype(BF16).astype(F32)
        terms.append(term)
        value = value - term
    return terms


def iota(shape, dim):
    return lax.broadcasted_iota(jnp.int32, shape, dim)


def places(value, size):
    bits = size.bit_length() - 1
    assert size == 1 << bits
    return value >> bits, value & (size - 1)


def pack_kernel(groups, per, source, cache_k, cache_v, out, src, kbuf, vbuf, in_sem, out_sem):
    loads = [
        pltpu.make_async_copy(a, b, in_sem.at[j])
        for j, (a, b) in enumerate(((source, src), (cache_k, kbuf), (cache_v, vbuf)))
    ]
    for copy in loads:
        copy.start()
    me = lax.axis_index("grp")
    loads[0].wait()
    picks = []
    for dest in range(groups):
        count = jnp.int32(0)
        chosen = [jnp.int32(0)] * MOVE
        for slot in range(per):
            owner, old = places(src[dest * per + slot], per)
            mine = (owner == me) & (me != dest)
            for rank in range(MOVE):
                chosen[rank] = jnp.where(mine & (count == rank), old, chosen[rank])
            count = count + mine.astype(jnp.int32)
        picks.append(chosen)
    stores = []
    for which, buf in ((0, kbuf), (1, vbuf)):
        loads[1 + which].wait()
        for dest in range(groups):
            for rank in range(MOVE):
                copy = pltpu.make_async_copy(
                    buf.at[picks[dest][rank]],
                    out.at[dest, which, rank],
                    out_sem.at[dest, which, rank],
                )
                copy.start()
                stores.append(copy)
    for copy in stores:
        copy.wait()


def column(values):
    rows = iota((len(values), 1), 0)
    result = jnp.zeros((len(values), 1), jnp.int32)
    for at, value in enumerate(values):
        result = jnp.where(rows == at, value, result)
    return result


def stay_kernel(
    groups, per, source, lengths, cache_k, cache_v, query, new_key, new_value, resid, gain, *refs
):
    (
    _, _, _, spare_valid, peaks, totals, contexts, start, gains, kbuf, vbuf, src, length, sems,
    ) = refs
    copies = [
        pltpu.make_async_copy(a, b, sems.at[j])
        for j, (a, b) in enumerate(
            ((source, src), (lengths, length), (cache_k, kbuf), (cache_v, vbuf))
        )
    ]
    for copy in copies:
        copy.start()
    me = lax.axis_index("grp")
    heads_kv, block = kbuf.shape[1], kbuf.shape[2]
    share = query.shape[0] // heads_kv
    base = lax.axis_index("dev") * block
    copies[0].wait()
    copies[1].wait()
    counts = [jnp.int32(0)] * groups
    spots, limits, arrivals = [], [], []
    for slot in range(per):
        owner = places(src[me * per + slot], per)[0]
        rank = jnp.int32(0)
        for g in range(groups):
            here = owner == g
            rank = jnp.where(here, counts[g], rank)
            counts[g] = counts[g] + here.astype(jnp.int32)
        spot = length[slot] - base
        spots.append(spot)
        limits.append(jnp.where(owner == me, spot, -1))
        arrivals.append(jnp.where(owner == me, -1, owner * MOVE + rank))
    spot, limit, arrival = column(spots), column(limits), column(arrivals)
    which, where = places(iota((per, per * block), 1), block)
    valid = (which == iota((per, per * block), 0)) & (where < limit)
    which, where = places(iota((per, groups * MOVE * block), 1), block)
    spare_valid[...] = ((which == arrival) & (where < spot)).astype(F32)
    fresh = (spot >= 0) & (spot < block)
    copies[2].wait()
    copies[3].wait()
    scale = LANES**-0.5
    for kv in range(heads_kv):
        keys = kbuf[:, kv].reshape(per * block, LANES)
        values = vbuf[:, kv].reshape(per * block, LANES)
        rows = query[kv * share : (kv + 1) * share]
        scores = lax.dot_general(
            rows.reshape(share * per, LANES), keys, (((1,), (1,)), ((), ())),
            preferred_element_type=F32,
        ).reshape(share, per, per * block) * scale
        scores = jnp.where(valid[None], scores, F32(-1e30))
        newest = jnp.sum(
            rows.astype(F32) * new_key[kv].astype(F32)[None], axis=-1, keepdims=True
        ) * scale
        newest = jnp.where(fresh[None], newest, F32(-1e30))
        peak = jnp.maximum(jnp.max(scores, axis=-1, keepdims=True), newest)
        weights = jnp.where(valid[None], jnp.exp(scores - peak), F32(0.0)).astype(BF16)
        added = jnp.where(fresh[None], jnp.exp(newest - peak), F32(0.0))
        total = jnp.sum(weights.astype(F32), axis=-1, keepdims=True) + added
        context = jnp.dot(
            weights.reshape(share * per, per * block), values, preferred_element_type=F32
        ).reshape(share, per, LANES) + added * new_value[kv].astype(F32)[None]
        at = slice(kv * share, (kv + 1) * share)
        peaks[at] = jnp.broadcast_to(peak, (share, per, LANES))
        totals[at] = jnp.broadcast_to(total, (share, per, LANES))
        contexts[at] = context
    dev = lax.axis_index("dev")
    even = dev % 2 == 0
    tiles = tiles_of(even, resid[...].astype(F32))
    lane = iota((1, LANES), 1)
    spare = (jnp.logical_not(even) & (lane < HALF), even & (lane >= HALF))
    for k in range(2):
        start[k] = tiles[k]
        at = 3 * (dev // 2) + dev % 2 + k
        own = jnp.where(iota(gain.shape, 0) == at, gain[...].astype(F32), F32(0.0))
        gains[k : k + 1] = jnp.where(spare[k], F32(0.0), jnp.sum(own, axis=0, keepdims=True))


def arrive_kernel(moved, query, spare_valid, peaks, totals, contexts, out):
    groups, _, _, heads_kv, block, _ = moved.shape
    share, per = query.shape[0] // heads_kv, query.shape[1]
    columns = groups * MOVE * block
    valid = spare_valid[...] > 0.5
    scale = LANES**-0.5
    ones = jnp.ones((columns, LANES), BF16)
    lane = iota((1, 1, LANES), 2)
    lane2 = iota((per, LANES), 1)
    first = ((lane2 >> 3) & 1) == 0
    low = lane2 < HALF
    for kv in range(heads_kv):
        keys = moved[:, 0, :, kv].reshape(columns, LANES)
        values = moved[:, 1, :, kv].reshape(columns, LANES)
        at = slice(kv * share, (kv + 1) * share)
        scores = lax.dot_general(
            query[at].reshape(share * per, LANES), keys, (((1,), (1,)), ((), ())),
            preferred_element_type=F32,
        ).reshape(share, per, columns) * scale
        scores = jnp.where(valid[None], scores, F32(-1e30))
        before = peaks[at]
        peak = jnp.maximum(before, jnp.max(scores, axis=-1, keepdims=True))
        whole = jnp.concatenate([peak] * (columns // LANES), axis=-1)
        weights = jnp.where(valid[None], jnp.exp(scores - whole), F32(0.0)).astype(BF16)
        keep = jnp.exp(before - peak)
        sums = jnp.dot(
            weights.reshape(share * per, columns),
            jnp.concatenate([values, ones], axis=1),
            preferred_element_type=F32,
        ).reshape(share, per, 2 * LANES)
        context = sums[..., :LANES] + keep * contexts[at]
        total = sums[..., LANES:] + keep * totals[at]
        stat = jnp.zeros((share, per, LANES), F32)
        for j, term in enumerate(pieces(peak, 3) + pieces(total, 2)):
            stat = jnp.where((lane & 7) == j, term, stat)
        for i in range(share // 3):
            m = kv * (share // 3) + i
            a, b, c = (context[3 * i + j] for j in range(3))
            sa, sb, sc = (stat[3 * i + j] for j in range(3))
            out[2 * m, 0] = a.astype(BF16)
            out[2 * m, 1] = jnp.where(low, b, jnp.where(first, sa, sb)).astype(BF16)
            out[2 * m + 1, 0] = jnp.where(low, jnp.where(first, sb, sc), b).astype(BF16)
            out[2 * m + 1, 1] = c.astype(BF16)


def store_kernel(
    groups, per, source, lengths, cache_k, cache_v, moved, new_key, new_value,
    out_k, out_v, kbuf, vbuf, src, length, small_sem, in_sem, out_sem,
):
    small = [
        pltpu.make_async_copy(source, src, small_sem.at[0]),
        pltpu.make_async_copy(lengths, length, small_sem.at[1]),
    ]
    for copy in small:
        copy.start()
    me = lax.axis_index("grp")
    heads_kv, block = kbuf.shape[1], kbuf.shape[2]
    base = lax.axis_index("dev") * block
    for copy in small:
        copy.wait()
    counts = [jnp.int32(0)] * groups
    for slot in range(per):
        owner = places(src[me * per + slot], per)[0]
        stays = owner == me
        rank = jnp.int32(0)
        for g in range(groups):
            here = owner == g
            rank = jnp.where(here, counts[g], rank)
            counts[g] = counts[g] + here.astype(jnp.int32)
        rank = jnp.minimum(rank, MOVE - 1)

        @pl.when(stays)
        def _():
            pltpu.make_async_copy(cache_k.at[slot], kbuf.at[slot], in_sem.at[0, slot]).start()
            pltpu.make_async_copy(cache_v.at[slot], vbuf.at[slot], in_sem.at[1, slot]).start()

        @pl.when(jnp.logical_not(stays))
        def _():
            pltpu.make_async_copy(moved.at[owner, 0, rank], kbuf.at[slot], in_sem.at[0, slot]).start()
            pltpu.make_async_copy(moved.at[owner, 1, rank], vbuf.at[slot], in_sem.at[1, slot]).start()

    outs = []
    for slot in range(per):
        pltpu.make_async_copy(cache_k.at[0], kbuf.at[slot], in_sem.at[0, slot]).wait()
        pltpu.make_async_copy(cache_v.at[0], vbuf.at[slot], in_sem.at[1, slot]).wait()
        spot = length[slot] - base

        @pl.when((spot >= 0) & (spot < block))
        def _():
            hit = iota((heads_kv, block, LANES), 1) == spot
            kbuf[slot] = jnp.where(hit, new_key[slot][:, None, :], kbuf[slot])
            vbuf[slot] = jnp.where(hit, new_value[slot][:, None, :], vbuf[slot])

        for which, buf, out in ((0, kbuf, out_k), (1, vbuf, out_v)):
            copy = pltpu.make_async_copy(buf.at[slot], out.at[slot], out_sem.at[which, slot])
            copy.start()
            outs.append(copy)
    for copy in outs:
        copy.wait()


def project_kernel(recv, weight, out, wbuf, w_sems):
    span = wbuf.shape[2]
    loads = []
    for j in range(wbuf.shape[0]):
        copy = pltpu.make_async_copy(
            weight.at[:, pl.ds(j * span, span)], wbuf.at[j], w_sems.at[j]
        )
        copy.start()
        loads.append(copy)
    even = lax.axis_index("dev") % 2 == 0
    per = recv.shape[2]
    peers = recv.shape[0]
    stat = jnp.where(even, recv[:, 1], recv[:, 0]).reshape(peers * per, LANES)
    kind, _ = places(iota((LANES, 4 * LANES), 1), LANES)
    term = iota((LANES, 4 * LANES), 0) - jnp.where(even, HALF, 0) - 8 * (kind >> 1)
    begin = 3 * (kind & 1)
    wanted = (term >= begin) & (term < 3 + 2 * (kind & 1))
    spread = jnp.dot(
        stat, wanted.astype(F32).astype(BF16), preferred_element_type=F32
    ).reshape(peers, per, 4 * LANES)
    parts = []
    for k in range(2):
        peak = spread[..., 2 * k * LANES : (2 * k + 1) * LANES]
        total = spread[..., (2 * k + 1) * LANES : (2 * k + 2) * LANES]
        factor = jnp.exp(peak - jnp.max(peak, axis=0, keepdims=True))
        whole = jnp.sum(factor * total, axis=0)
        parts.append(jnp.sum(factor * recv[:, k].astype(F32), axis=0) / whole)
    both = jnp.concatenate(parts, axis=1)
    rows = weight.shape[0]
    attn = jnp.where(even, both[:, :rows], both[:, 2 * LANES - rows :]).astype(BF16)
    for m in range(out.shape[0] // 2):
        j, at = divmod(3 * LANES * m, span)
        if at == 0:
            loads[j].wait()
        part = jnp.dot(
            attn, wbuf[j, :, at : at + 3 * LANES], preferred_element_type=F32
        ).astype(BF16)
        t0, t1, t2 = (part[:, LANES * j : LANES * (j + 1)] for j in range(3))
        out[2 * m, 0] = t0
        out[2 * m, 1] = t1
        out[2 * m + 1, 0] = t1
        out[2 * m + 1, 1] = t2


def tiles_of(even, wide):
    rows = wide.shape[0]
    zero = jnp.zeros((rows, HALF), wide.dtype)
    left = jnp.concatenate([wide, zero], axis=1)
    right = jnp.concatenate([zero, wide], axis=1)
    both = jnp.where(even, left, right)
    return both[:, :LANES], both[:, LANES:]


def dispatch_kernel(recv, start, gains, qrow, mixed, out):
    even = lax.axis_index("dev") % 2 == 0
    per = recv.shape[2]
    lane = iota((per, LANES), 1)
    spare = (jnp.logical_not(even) & (lane < HALF), even & (lane >= HALF))
    square = jnp.zeros((per, 1), F32)
    wides = []
    for k in range(2):
        part = start[k] + jnp.sum(recv[:, k].astype(F32), axis=0)
        part = jnp.where(spare[k], F32(0.0), part)
        mixed[k] = part
        square = square + jnp.sum(part * part, axis=1, keepdims=True)
        wides.append(part * gains[k : k + 1])
    stat = jnp.zeros((per, LANES), F32)
    for at, term in enumerate(pieces(square, 3)):
        stat = jnp.where((lane & 7) == at, term, stat)
    rows = jnp.concatenate(
        [jnp.where(spare[k], stat, wides[k]).astype(BF16) for k in range(2)], axis=0
    )
    count = EXPERTS * 2 * CAP
    where = iota((count, 2 * per), 0)
    from_ = iota((count, 2 * per), 1)
    expert, _ = places(where, 2 * CAP)
    half, place = places(where, CAP)
    slot = expert * CAP + place
    named = (slot == qrow[0:1, :]) | (slot == qrow[1:2, :])
    pick = (named & ((half & 1) == places(from_, per)[0])).astype(F32).astype(BF16)
    sent = jnp.dot(pick, rows, preferred_element_type=F32).astype(BF16)
    split = out.shape[0] // EXPERTS
    for e in range(EXPERTS):
        block = sent[2 * CAP * e : 2 * CAP * (e + 1)]
        for s in range(split):
            out[e * split + s] = block


def expert_kernel(groups, recv, w_gate, w_up, w_down, out, xbuf, buf, wg, wu, wd, w_sems, sems):
    width = xbuf.shape[1]
    depth, span = wg.shape[1], wd.shape[2]
    firsts, seconds = [], []
    for j in range(wg.shape[0]):
        rows = pl.ds(j * depth, depth)
        pair = (
            pltpu.make_async_copy(w_gate.at[rows], wg.at[j], w_sems.at[0, j]),
            pltpu.make_async_copy(w_up.at[rows], wu.at[j], w_sems.at[1, j]),
        )
        for copy in pair:
            copy.start()
        firsts.append(pair)
    for j in range(wd.shape[0]):
        copy = pltpu.make_async_copy(
            w_down.at[:, pl.ds(j * span, span)], wd.at[j], w_sems.at[2, j]
        )
        copy.start()
        seconds.append(copy)
    devs = recv.shape[0] // groups
    lane = iota((CAP, LANES), 1)
    low = lane < HALF
    rows_square = []
    for g in range(groups):
        acc = jnp.zeros((CAP, LANES), F32)
        for m in range(devs // 2):
            e, o = recv[g * devs + 2 * m], recv[g * devs + 2 * m + 1]
            middle_e, middle_o = e[CAP:].astype(F32), o[:CAP].astype(F32)
            acc = acc + jnp.where(low, middle_o, middle_e)
            at = slice(CAP * g, CAP * (g + 1))
            xbuf[at, 3 * LANES * m : 3 * LANES * m + LANES] = e[:CAP]
            xbuf[at, 3 * LANES * m + LANES : 3 * LANES * m + 2 * LANES] = jnp.where(
                low, middle_e, middle_o
            ).astype(BF16)
            xbuf[at, 3 * LANES * m + 2 * LANES : 3 * LANES * (m + 1)] = o[CAP:]
        both = acc[:, :8] + acc[:, HALF : HALF + 8]
        rows_square.append(both[:, 0:1] + both[:, 1:2] + both[:, 2:3])
    square = jnp.concatenate(rows_square, axis=0)
    scale = lax.rsqrt(square / width + 1e-05)
    gate = jnp.zeros((groups * CAP, wg.shape[2]), F32)
    up = jnp.zeros((groups * CAP, wu.shape[2]), F32)
    for j, pair in enumerate(firsts):
        x = xbuf[:, depth * j : depth * (j + 1)]
        pair[0].wait()
        gate = gate + jnp.dot(x, wg[j], preferred_element_type=F32)
        pair[1].wait()
        up = up + jnp.dot(x, wu[j], preferred_element_type=F32)
    gate, up = gate * scale, up * scale
    hidden = (gate / (1.0 + jnp.exp(-gate)) * up).astype(BF16)
    copies = []
    for m in range(devs // 2):
        j, at = divmod(3 * LANES * m, span)
        if at == 0:
            seconds[j].wait()
        part = jnp.dot(
            hidden, wd[j, :, at : at + 3 * LANES], preferred_element_type=F32
        )
        t = [part[:, LANES * k : LANES * (k + 1)] for k in range(3)]
        for g in range(groups):
            at = slice(CAP * g, CAP * (g + 1))
            for i in range(2):
                buf[g, 2 * m + i] = jnp.concatenate([t[i][at], t[i + 1][at]], axis=0).astype(BF16)
            copy = pltpu.make_async_copy(
                buf.at[g, pl.ds(2 * m, 2)], out.at[pl.ds(g * devs + 2 * m, 2)], sems.at[g, m]
            )
            copy.start()
            copies.append(copy)
    for copy in copies:
        copy.wait()


def final_kernel(recv, mixed, qcol, share, out):
    even = lax.axis_index("dev") % 2 == 0
    split = recv.shape[0] // EXPERTS
    per = mixed.shape[1]
    sums = [
        jnp.sum(recv[e * split : (e + 1) * split].astype(F32), axis=0) for e in range(EXPERTS)
    ]
    slot = iota((per, EXPERTS * CAP), 1)
    weight = jnp.where(slot == qcol[:, 0:1], share[:, 0:1], F32(0.0)) + jnp.where(
        slot == qcol[:, 1:2], share[:, 1:2], F32(0.0)
    )
    done = []
    for k in range(2):
        expert = jnp.concatenate([s[CAP * k : CAP * (k + 1)] for s in sums], axis=0)
        moe = jnp.dot(
            weight, expert, preferred_element_type=F32, precision=lax.Precision.HIGHEST
        )
        done.append(mixed[k] + moe)
    both = jnp.concatenate(done, axis=1)
    width = out.shape[1]
    out[...] = jnp.where(even, both[:, :width], both[:, 2 * LANES - width :]).astype(BF16)


def params(free):
    return pltpu.CompilerParams(vmem_limit_bytes=67043328 - free)


def on_device(
    cache_k,
    cache_v,
    source,
    lengths,
    query,
    new_key,
    new_value,
    resid,
    out_weight,
    norm_gain,
    w_gate,
    w_up,
    w_down,
    expert_ids,
    gate_codes,
):
    groups = lax.axis_size("grp")
    devs = lax.axis_size("dev")
    per, kv_heads, block, head_dim = cache_k.shape
    heads = query.shape[1] // head_dim
    width = query.shape[1]
    hidden = w_gate.shape[1]
    sds = jax.ShapeDtypeStruct
    cache_k, cache_v, source, lengths, out_weight, w_gate, w_up, w_down = (
        pltpu.with_memory_space_constraint(a, pltpu.HBM)
        for a in (cache_k, cache_v, source, lengths, out_weight, w_gate, w_up, w_down)
    )
    move_shape = (groups, 2, MOVE, kv_heads, block, head_dim)

    sent = pl.pallas_call(
        functools.partial(pack_kernel, groups, per),
        name="pack",
        out_shape=sds(move_shape, BF16),
        in_specs=[HBM, HBM, HBM],
        out_specs=HBM,
        scratch_shapes=[
            pltpu.SMEM(source.shape, jnp.int32),
            pltpu.VMEM(cache_k.shape, BF16),
            pltpu.VMEM(cache_v.shape, BF16),
            pltpu.SemaphoreType.DMA((3,)),
            pltpu.SemaphoreType.DMA((groups, 2, MOVE)),
        ],
        compiler_params=params(56 << 20),
    )(source, cache_k, cache_v)
    moved = lax.all_to_all(sent, "grp", split_axis=0, concat_axis=0, tiled=True)

    flat = expert_ids.reshape(-1)
    order = jnp.arange(flat.shape[0], dtype=jnp.int32)
    same = (flat[:, None] == flat[None, :]) & (order[None, :] < order[:, None])
    qflat = flat * CAP + jnp.sum(same.astype(jnp.int32), axis=1)
    qcol = qflat.reshape(per, 2)
    qrow = jnp.concatenate([qcol.T, qcol.T], axis=1)
    codes = gate_codes.astype(F32)
    share = codes / jnp.sum(codes, axis=-1, keepdims=True)
    by_head = query.reshape(per, heads, head_dim).transpose(1, 0, 2)

    row_shape = sds((heads, per, LANES), F32)
    spare_valid, peaks, totals, contexts, start, gains = pl.pallas_call(
        functools.partial(stay_kernel, groups, per),
        name="stay",
        out_shape=(
            sds((per, groups * MOVE * block), F32),
            row_shape,
            row_shape,
            row_shape,
            sds((2, per, LANES), F32),
            sds((2, LANES), F32),
        ),
        in_specs=[HBM] * 4 + [VMEM] * 8,
        out_specs=(VMEM,) * 6,
        scratch_shapes=[
            pltpu.VMEM(cache_k.shape, BF16),
            pltpu.VMEM(cache_v.shape, BF16),
            pltpu.SMEM(source.shape, jnp.int32),
            pltpu.SMEM(lengths.shape, jnp.int32),
            pltpu.SemaphoreType.DMA((4,)),
        ],
        compiler_params=params(48 << 20),
        cost_estimate=pl.CostEstimate(flops=0, transcendentals=0, bytes_accessed=16 << 20),
    )(
        source, lengths, cache_k, cache_v, by_head,
        new_key.transpose(1, 0, 2), new_value.transpose(1, 0, 2), resid,
        norm_gain.reshape(-1, LANES), qrow, qcol, share,
    )

    ctx = pl.pallas_call(
        arrive_kernel,
        name="arrive",
        out_shape=sds((devs, 2, per, LANES), BF16),
        in_specs=[VMEM] * 6,
        out_specs=VMEM,
        compiler_params=params(52 << 20),
    )(moved, by_head, spare_valid, peaks, totals, contexts)
    ctx = lax.all_to_all(ctx, "dev", split_axis=0, concat_axis=0, tiled=True)

    new_k, new_v = pl.pallas_call(
        functools.partial(store_kernel, groups, per),
        name="store",
        out_shape=(sds(cache_k.shape, BF16), sds(cache_v.shape, BF16)),
        in_specs=[HBM, HBM, HBM, HBM, pl.BlockSpec(memory_space=pl.ANY), VMEM, VMEM],
        out_specs=(HBM, HBM),
        scratch_shapes=[
            pltpu.VMEM(cache_k.shape, BF16),
            pltpu.VMEM(cache_v.shape, BF16),
            pltpu.SMEM(source.shape, jnp.int32),
            pltpu.SMEM(lengths.shape, jnp.int32),
            pltpu.SemaphoreType.DMA((2,)),
            pltpu.SemaphoreType.DMA((2, per)),
            pltpu.SemaphoreType.DMA((2, per)),
        ],
        compiler_params=params(52 << 20),
        cost_estimate=pl.CostEstimate(flops=0, transcendentals=0, bytes_accessed=8 << 20),
    )(source, lengths, cache_k, cache_v, moved, new_key, new_value)

    partial_rows = pl.pallas_call(
        project_kernel,
        name="project",
        out_shape=sds((devs, 2, per, LANES), BF16),
        in_specs=[VMEM, HBM],
        out_specs=VMEM,
        scratch_shapes=[
            pltpu.VMEM((8, out_weight.shape[0], width // 8), BF16),
            pltpu.SemaphoreType.DMA((8,)),
        ],
        compiler_params=params(52 << 20),
    )(ctx, out_weight)
    partial_rows = lax.all_to_all(partial_rows, "dev", split_axis=0, concat_axis=0, tiled=True)

    mixed, rows = pl.pallas_call(
        dispatch_kernel,
        name="dispatch",
        out_shape=(
            sds((2, per, LANES), F32),
            sds((groups * devs, 2 * CAP, LANES), BF16),
        ),
        in_specs=[VMEM] * 4,
        out_specs=(VMEM, VMEM),
        compiler_params=params(56 << 20),
    )(partial_rows, start, gains, qrow)
    rows = lax.all_to_all(rows, ("grp", "dev"), split_axis=0, concat_axis=0, tiled=True)

    chunks, down_chunks = 12, 8
    partial_out = pl.pallas_call(
        functools.partial(expert_kernel, groups),
        name="expert",
        out_shape=sds((groups * devs, 2 * CAP, LANES), BF16),
        in_specs=[VMEM, HBM, HBM, HBM],
        out_specs=HBM,
        scratch_shapes=[
            pltpu.VMEM((groups * CAP, width), BF16),
            pltpu.VMEM((groups, devs, 2 * CAP, LANES), BF16),
            pltpu.VMEM((chunks, width // chunks, hidden), BF16),
            pltpu.VMEM((chunks, width // chunks, hidden), BF16),
            pltpu.VMEM((down_chunks, hidden, width // down_chunks), BF16),
            pltpu.SemaphoreType.DMA((3, chunks)),
            pltpu.SemaphoreType.DMA((groups, devs // 2)),
        ],
        compiler_params=params(32 << 20),
    )(rows, w_gate, w_up, w_down)
    partial_out = lax.all_to_all(
        partial_out, ("grp", "dev"), split_axis=0, concat_axis=0, tiled=True
    )

    layer_out = pl.pallas_call(
        final_kernel,
        name="final",
        out_shape=sds(resid.shape, BF16),
        in_specs=[VMEM] * 4,
        out_specs=VMEM,
        compiler_params=params(56 << 20),
    )(partial_out, mixed, qcol, share)
    return (new_k, new_v, layer_out)


def solution(mesh):
    in_specs = (
        P("grp", None, "dev", None),
        P("grp", None, "dev", None),
        P(),
        P("grp"),
        P("grp", None),
        P("grp", None, None),
        P("grp", None, None),
        P("grp", "dev"),
        P("dev", None),
        P(),
        P(None, ("grp", "dev")),
        P(None, ("grp", "dev")),
        P(("grp", "dev"), None),
        P("grp", None),
        P("grp", None),
    )
    out_specs = (P("grp", None, "dev", None), P("grp", None, "dev", None), P("grp", "dev"))
    return jax.shard_map(
        on_device, mesh=mesh, in_specs=in_specs, out_specs=out_specs, check_vma=False
    )
```

```python
import functools

import jax
import jax.numpy as jnp
from jax import lax
from jax.experimental import pallas as pl
from jax.experimental.pallas import tpu as pltpu
from jax.sharding import PartitionSpec as P

EXPERTS = 8
MOVE = 2
CAP = 8
LANES = 128
HALF = 64
ORDER = (1, 0, 3, 2)
F32 = jnp.float32
BF16 = jnp.bfloat16
VMEM = pl.BlockSpec(memory_space=pltpu.VMEM)
SMEM = pl.BlockSpec(memory_space=pltpu.SMEM)
HBM = pl.BlockSpec(memory_space=pltpu.HBM)


def pieces(value, count):
    terms = []
    for _ in range(count):
        term = value.astype(BF16).astype(F32)
        terms.append(term)
        value = value - term
    return terms


def iota(shape, dim):
    return lax.broadcasted_iota(jnp.int32, shape, dim)


def places(value, size):
    bits = size.bit_length() - 1
    assert size == 1 << bits
    return value >> bits, value & (size - 1)


def sendings(groups):
    plan = []
    for step in range(1, groups):
        if 1 < step < groups - 1:
            plan += [(step, (rank,)) for rank in range(MOVE)]
        else:
            plan.append((step, tuple(range(MOVE))))
    return plan


def pack_kernel(groups, per, source, cache_k, cache_v, *refs):
    outs, (src, kbuf, vbuf, in_sem, out_sem) = refs[:-5], refs[-5:]
    loads = [
        pltpu.make_async_copy(a, b, in_sem.at[j])
        for j, (a, b) in enumerate(((source, src), (cache_k, kbuf), (cache_v, vbuf)))
    ]
    for copy in loads:
        copy.start()
    me = lax.axis_index("grp")
    loads[0].wait()
    picks = []
    for step in range(1, groups):
        dest = lax.rem(me + step, groups)
        count = jnp.int32(0)
        chosen = [jnp.int32(0)] * MOVE
        for slot in range(per):
            owner, old = places(src[dest * per + slot], per)
            mine = owner == me
            for rank in range(MOVE):
                chosen[rank] = jnp.where(mine & (count == rank), old, chosen[rank])
            count = count + mine.astype(jnp.int32)
        picks.append(chosen)
    stores = []
    for which, buf in ((0, kbuf), (1, vbuf)):
        loads[1 + which].wait()
        for at, (out, (step, ranks)) in enumerate(zip(outs, sendings(groups))):
            for j, rank in enumerate(ranks):
                copy = pltpu.make_async_copy(
                    buf.at[picks[step - 1][rank]], out.at[which, j], out_sem.at[at, which, j]
                )
                copy.start()
                stores.append(copy)
    for copy in stores:
        copy.wait()


def column(values):
    rows = iota((len(values), 1), 0)
    result = jnp.zeros((len(values), 1), jnp.int32)
    for at, value in enumerate(values):
        result = jnp.where(rows == at, value, result)
    return result


def stay_kernel(
    groups, per, source, lengths, cache_k, cache_v, query, new_key, new_value, resid, gain, *refs
):
    (
        _, spare_valid, peaks, totals, contexts, start, gains,
        kbuf, vbuf, src, length, nk, nv, own_resid, gain_all, sems,
    ) = refs
    copies = [
        pltpu.make_async_copy(a, b, sems.at[j])
        for j, (a, b) in enumerate(
            (
                (source, src), (lengths, length), (cache_k, kbuf), (cache_v, vbuf),
                (new_key, nk), (new_value, nv), (resid, own_resid), (gain, gain_all),
            )
        )
    ]
    for copy in copies:
        copy.start()
    me = lax.axis_index("grp")
    heads_kv, block = kbuf.shape[1], kbuf.shape[2]
    share = query.shape[0] // heads_kv
    base = lax.axis_index("dev") * block
    copies[0].wait()
    copies[1].wait()
    counts = [jnp.int32(0)] * groups
    spots, limits, arrivals = [], [], []
    for slot in range(per):
        owner = places(src[me * per + slot], per)[0]
        rank = jnp.int32(0)
        for g in range(groups):
            here = owner == g
            rank = jnp.where(here, counts[g], rank)
            counts[g] = counts[g] + here.astype(jnp.int32)
        spot = length[slot] - base
        spots.append(spot)
        limits.append(jnp.where(owner == me, spot, -1))
        ahead = lax.rem(me - owner + groups, groups)
        arrivals.append(jnp.where(owner == me, -1, (ahead - 1) * MOVE + rank))
    spot, limit, arrival = column(spots), column(limits), column(arrivals)
    which, where = places(iota((per, per * block), 1), block)
    valid = (which == iota((per, per * block), 0)) & (where < limit)
    which, where = places(iota((per, groups * MOVE * block), 1), block)
    spare_valid[...] = ((which == arrival) & (where < spot)).astype(F32)
    fresh = (spot >= 0) & (spot < block)
    for copy in copies[2:]:
        copy.wait()
    new_keys, new_values = nk[...].astype(F32), nv[...].astype(F32)
    scale = LANES**-0.5
    for kv in range(heads_kv):
        keys = kbuf[:, kv].reshape(per * block, LANES)
        values = vbuf[:, kv].reshape(per * block, LANES)
        rows = query[kv * share : (kv + 1) * share]
        scores = lax.dot_general(
            rows.reshape(share * per, LANES), keys, (((1,), (1,)), ((), ())),
            preferred_element_type=F32,
        ).reshape(share, per, per * block) * scale
        scores = jnp.where(valid[None], scores, F32(-1e30))
        newest = jnp.sum(
            rows.astype(F32) * new_keys[:, kv][None], axis=-1, keepdims=True
        ) * scale
        newest = jnp.where(fresh[None], newest, F32(-1e30))
        peak = jnp.maximum(jnp.max(scores, axis=-1, keepdims=True), newest)
        weights = jnp.where(valid[None], jnp.exp(scores - peak), F32(0.0)).astype(BF16)
        added = jnp.where(fresh[None], jnp.exp(newest - peak), F32(0.0))
        total = jnp.sum(weights.astype(F32), axis=-1, keepdims=True) + added
        context = jnp.dot(
            weights.reshape(share * per, per * block), values, preferred_element_type=F32
        ).reshape(share, per, LANES) + added * new_values[:, kv][None]
        at = slice(kv * share, (kv + 1) * share)
        peaks[at] = jnp.broadcast_to(peak, (share, per, LANES))
        totals[at] = jnp.broadcast_to(total, (share, per, LANES))
        contexts[at] = context
    dev = lax.axis_index("dev")
    even = dev % 2 == 0
    tiles = tiles_of(even, own_resid[...].astype(F32))
    lane = iota((1, LANES), 1)
    spare = (jnp.logical_not(even) & (lane < HALF), even & (lane >= HALF))
    for k in range(2):
        start[k] = tiles[k]
        at = 3 * (dev // 2) + dev % 2 + k
        own = jnp.where(iota(gain.shape, 0) == at, gain_all[...].astype(F32), F32(0.0))
        gains[k : k + 1] = jnp.where(spare[k], F32(0.0), jnp.sum(own, axis=0, keepdims=True))


def arrive_kernel(query, spare_valid, peaks, totals, contexts, *refs):
    moved, out = refs[:-1], refs[-1]
    heads_kv, block = moved[0].shape[2:4]
    share, per = query.shape[0] // heads_kv, query.shape[1]
    columns = spare_valid.shape[1]

    def gather(which, kv):
        blocks = [m[which, j, kv] for m in moved for j in range(m.shape[1])]
        spare = columns // block - len(blocks)
        return jnp.concatenate(blocks + blocks[:spare], axis=0)

    valid = spare_valid[...] > 0.5
    scale = LANES**-0.5
    ones = jnp.ones((columns, LANES), BF16)
    lane = iota((1, 1, LANES), 2)
    lane2 = iota((per, LANES), 1)
    first = ((lane2 >> 3) & 1) == 0
    low = lane2 < HALF
    for kv in range(heads_kv):
        keys, values = gather(0, kv), gather(1, kv)
        at = slice(kv * share, (kv + 1) * share)
        scores = lax.dot_general(
            query[at].reshape(share * per, LANES), keys, (((1,), (1,)), ((), ())),
            preferred_element_type=F32,
        ).reshape(share, per, columns) * scale
        scores = jnp.where(valid[None], scores, F32(-1e30))
        before = peaks[at]
        peak = jnp.maximum(before, jnp.max(scores, axis=-1, keepdims=True))
        whole = jnp.concatenate([peak] * (columns // LANES), axis=-1)
        weights = jnp.where(valid[None], jnp.exp(scores - whole), F32(0.0)).astype(BF16)
        keep = jnp.exp(before - peak)
        sums = jnp.dot(
            weights.reshape(share * per, columns),
            jnp.concatenate([values, ones], axis=1),
            preferred_element_type=F32,
        ).reshape(share, per, 2 * LANES)
        context = sums[..., :LANES] + keep * contexts[at]
        total = sums[..., LANES:] + keep * totals[at]
        stat = jnp.zeros((share, per, LANES), F32)
        for j, term in enumerate(pieces(peak, 3) + pieces(total, 2)):
            stat = jnp.where((lane & 7) == j, term, stat)
        for i in range(share // 3):
            m = kv * (share // 3) + i
            a, b, c = (context[3 * i + j] for j in range(3))
            sa, sb, sc = (stat[3 * i + j] for j in range(3))
            out[2 * m, 0] = a.astype(BF16)
            out[2 * m, 1] = jnp.where(low, b, jnp.where(first, sa, sb)).astype(BF16)
            out[2 * m + 1, 0] = jnp.where(low, jnp.where(first, sb, sc), b).astype(BF16)
            out[2 * m + 1, 1] = c.astype(BF16)


def store_kernel(
    groups, per, source, lengths, cache_k, cache_v, new_key, new_value, *refs
):
    moved = refs[:-9]
    out_k, out_v, kbuf, vbuf, src, length, small_sem, in_sem, out_sem = refs[-9:]
    small = [
        pltpu.make_async_copy(source, src, small_sem.at[0]),
        pltpu.make_async_copy(lengths, length, small_sem.at[1]),
    ]
    for copy in small:
        copy.start()
    me = lax.axis_index("grp")
    heads_kv, block = kbuf.shape[1], kbuf.shape[2]
    base = lax.axis_index("dev") * block
    for copy in small:
        copy.wait()
    counts = [jnp.int32(0)] * groups
    for slot in range(per):
        owner = places(src[me * per + slot], per)[0]
        stays = owner == me
        rank = jnp.int32(0)
        for g in range(groups):
            here = owner == g
            rank = jnp.where(here, counts[g], rank)
            counts[g] = counts[g] + here.astype(jnp.int32)
        rank = jnp.minimum(rank, MOVE - 1)

        @pl.when(stays)
        def _():
            pltpu.make_async_copy(cache_k.at[slot], kbuf.at[slot], in_sem.at[0, slot]).start()
            pltpu.make_async_copy(cache_v.at[slot], vbuf.at[slot], in_sem.at[1, slot]).start()

        ahead = lax.rem(me - owner + groups, groups)
        for piece, (step, ranks) in zip(moved, sendings(groups)):
            for j, chosen in enumerate(ranks):

                @pl.when((ahead == step) & (rank == chosen))
                def _():
                    pltpu.make_async_copy(piece.at[0, j], kbuf.at[slot], in_sem.at[0, slot]).start()
                    pltpu.make_async_copy(piece.at[1, j], vbuf.at[slot], in_sem.at[1, slot]).start()

    outs = []
    for slot in range(per):
        pltpu.make_async_copy(cache_k.at[0], kbuf.at[slot], in_sem.at[0, slot]).wait()
        pltpu.make_async_copy(cache_v.at[0], vbuf.at[slot], in_sem.at[1, slot]).wait()
        spot = length[slot] - base

        @pl.when((spot >= 0) & (spot < block))
        def _():
            hit = iota((heads_kv, block, LANES), 1) == spot
            kbuf[slot] = jnp.where(hit, new_key[slot][:, None, :], kbuf[slot])
            vbuf[slot] = jnp.where(hit, new_value[slot][:, None, :], vbuf[slot])

        for which, buf, out in ((0, kbuf, out_k), (1, vbuf, out_v)):
            copy = pltpu.make_async_copy(buf.at[slot], out.at[slot], out_sem.at[which, slot])
            copy.start()
            outs.append(copy)
    for copy in outs:
        copy.wait()


def project_kernel(recv, weight, out, wbuf, w_sems):
    span = wbuf.shape[2]
    loads = []
    for j in range(wbuf.shape[0]):
        copy = pltpu.make_async_copy(
            weight.at[:, pl.ds(j * span, span)], wbuf.at[j], w_sems.at[j]
        )
        copy.start()
        loads.append(copy)
    even = lax.axis_index("dev") % 2 == 0
    per = recv.shape[2]
    peers = recv.shape[0]
    stat = jnp.where(even, recv[:, 1], recv[:, 0]).reshape(peers * per, LANES)
    kind, _ = places(iota((LANES, 4 * LANES), 1), LANES)
    term = iota((LANES, 4 * LANES), 0) - jnp.where(even, HALF, 0) - 8 * (kind >> 1)
    begin = 3 * (kind & 1)
    wanted = (term >= begin) & (term < 3 + 2 * (kind & 1))
    spread = jnp.dot(
        stat, wanted.astype(F32).astype(BF16), preferred_element_type=F32
    ).reshape(peers, per, 4 * LANES)
    parts = []
    for k in range(2):
        peak = spread[..., 2 * k * LANES : (2 * k + 1) * LANES]
        total = spread[..., (2 * k + 1) * LANES : (2 * k + 2) * LANES]
        factor = jnp.exp(peak - jnp.max(peak, axis=0, keepdims=True))
        whole = jnp.sum(factor * total, axis=0)
        parts.append(jnp.sum(factor * recv[:, k].astype(F32), axis=0) / whole)
    both = jnp.concatenate(parts, axis=1)
    rows = weight.shape[0]
    attn = jnp.where(even, both[:, :rows], both[:, 2 * LANES - rows :]).astype(BF16)
    for m in range(out.shape[0] // 2):
        j, at = divmod(3 * LANES * m, span)
        if at == 0:
            loads[j].wait()
        part = jnp.dot(
            attn, wbuf[j, :, at : at + 3 * LANES], preferred_element_type=F32
        ).astype(BF16)
        t0, t1, t2 = (part[:, LANES * j : LANES * (j + 1)] for j in range(3))
        out[2 * m, 0] = t0
        out[2 * m, 1] = t1
        out[2 * m + 1, 0] = t1
        out[2 * m + 1, 1] = t2


def tiles_of(even, wide):
    rows = wide.shape[0]
    zero = jnp.zeros((rows, HALF), wide.dtype)
    left = jnp.concatenate([wide, zero], axis=1)
    right = jnp.concatenate([zero, wide], axis=1)
    both = jnp.where(even, left, right)
    return both[:, :LANES], both[:, LANES:]


def dispatch_kernel(recv, start, gains, qrow, mixed, out):
    even = lax.axis_index("dev") % 2 == 0
    per = recv.shape[2]
    lane = iota((per, LANES), 1)
    spare = (jnp.logical_not(even) & (lane < HALF), even & (lane >= HALF))
    square = jnp.zeros((per, 1), F32)
    wides = []
    for k in range(2):
        part = start[k] + jnp.sum(recv[:, k].astype(F32), axis=0)
        part = jnp.where(spare[k], F32(0.0), part)
        mixed[k] = part
        square = square + jnp.sum(part * part, axis=1, keepdims=True)
        wides.append(part * gains[k : k + 1])
    stat = jnp.zeros((per, LANES), F32)
    for at, term in enumerate(pieces(square, 3)):
        stat = jnp.where((lane & 7) == at, term, stat)
    rows = jnp.concatenate(
        [jnp.where(spare[k], stat, wides[k]).astype(BF16) for k in range(2)], axis=0
    )
    count = EXPERTS * 2 * CAP
    where = iota((count, 2 * per), 0)
    from_ = iota((count, 2 * per), 1)
    expert, _ = places(where, 2 * CAP)
    half, place = places(where, CAP)
    slot = expert * CAP + place
    named = (slot == qrow[0:1, :]) | (slot == qrow[1:2, :])
    pick = (named & ((half & 1) == places(from_, per)[0])).astype(F32).astype(BF16)
    sent = jnp.dot(pick, rows, preferred_element_type=F32).astype(BF16)
    split = out.shape[0] // EXPERTS
    for e in range(EXPERTS):
        block = sent[2 * CAP * e : 2 * CAP * (e + 1)]
        for s in range(split):
            out[e * split + s] = block


def expert_kernel(groups, recv, w_gate, w_up, w_down, out, xbuf, buf, wg, wu, wd, w_sems, sems):
    width = xbuf.shape[1]
    depth, span = wg.shape[1], wd.shape[2]
    firsts, seconds = [], []
    for j in range(wg.shape[0]):
        rows = pl.ds(j * depth, depth)
        pair = (
            pltpu.make_async_copy(w_gate.at[rows], wg.at[j], w_sems.at[0, j]),
            pltpu.make_async_copy(w_up.at[rows], wu.at[j], w_sems.at[1, j]),
        )
        for copy in pair:
            copy.start()
        firsts.append(pair)
    for j in range(wd.shape[0]):
        copy = pltpu.make_async_copy(
            w_down.at[:, pl.ds(j * span, span)], wd.at[j], w_sems.at[2, j]
        )
        copy.start()
        seconds.append(copy)
    devs = recv.shape[0] // groups
    lane = iota((CAP, LANES), 1)
    low = lane < HALF
    rows_square = []
    for g in range(groups):
        acc = jnp.zeros((CAP, LANES), F32)
        for m in range(devs // 2):
            e, o = recv[g * devs + 2 * m], recv[g * devs + 2 * m + 1]
            middle_e, middle_o = e[CAP:].astype(F32), o[:CAP].astype(F32)
            acc = acc + jnp.where(low, middle_o, middle_e)
            at = slice(CAP * g, CAP * (g + 1))
            xbuf[at, 3 * LANES * m : 3 * LANES * m + LANES] = e[:CAP]
            xbuf[at, 3 * LANES * m + LANES : 3 * LANES * m + 2 * LANES] = jnp.where(
                low, middle_e, middle_o
            ).astype(BF16)
            xbuf[at, 3 * LANES * m + 2 * LANES : 3 * LANES * (m + 1)] = o[CAP:]
        both = acc[:, :8] + acc[:, HALF : HALF + 8]
        rows_square.append(both[:, 0:1] + both[:, 1:2] + both[:, 2:3])
    square = jnp.concatenate(rows_square, axis=0)
    scale = lax.rsqrt(square / width + 1e-05)
    gate = jnp.zeros((groups * CAP, wg.shape[2]), F32)
    up = jnp.zeros((groups * CAP, wu.shape[2]), F32)
    for j, pair in enumerate(firsts):
        x = xbuf[:, depth * j : depth * (j + 1)]
        pair[0].wait()
        gate = gate + jnp.dot(x, wg[j], preferred_element_type=F32)
        pair[1].wait()
        up = up + jnp.dot(x, wu[j], preferred_element_type=F32)
    gate, up = gate * scale, up * scale
    hidden = (gate / (1.0 + jnp.exp(-gate)) * up).astype(BF16)
    copies = []
    for m in range(devs // 2):
        j, at = divmod(3 * LANES * m, span)
        if at == 0:
            seconds[j].wait()
        part = jnp.dot(
            hidden, wd[j, :, at : at + 3 * LANES], preferred_element_type=F32
        )
        t = [part[:, LANES * k : LANES * (k + 1)] for k in range(3)]
        for g in range(groups):
            at = slice(CAP * g, CAP * (g + 1))
            for i in range(2):
                buf[g, 2 * m + i] = jnp.concatenate([t[i][at], t[i + 1][at]], axis=0).astype(BF16)
            copy = pltpu.make_async_copy(
                buf.at[g, pl.ds(2 * m, 2)], out.at[pl.ds(g * devs + 2 * m, 2)], sems.at[g, m]
            )
            copy.start()
            copies.append(copy)
    for copy in copies:
        copy.wait()


def final_kernel(recv, mixed, qcol, share, out):
    even = lax.axis_index("dev") % 2 == 0
    split = recv.shape[0] // EXPERTS
    per = mixed.shape[1]
    sums = [
        jnp.sum(recv[e * split : (e + 1) * split].astype(F32), axis=0) for e in range(EXPERTS)
    ]
    slot = iota((per, EXPERTS * CAP), 1)
    weight = jnp.where(slot == qcol[:, 0:1], share[:, 0:1], F32(0.0)) + jnp.where(
        slot == qcol[:, 1:2], share[:, 1:2], F32(0.0)
    )
    done = []
    for k in range(2):
        expert = jnp.concatenate([s[CAP * k : CAP * (k + 1)] for s in sums], axis=0)
        moe = jnp.dot(
            weight, expert, preferred_element_type=F32, precision=lax.Precision.HIGHEST
        )
        done.append(mixed[k] + moe)
    both = jnp.concatenate(done, axis=1)
    width = out.shape[1]
    out[...] = jnp.where(even, both[:, :width], both[:, 2 * LANES - width :]).astype(BF16)


def params(free):
    return pltpu.CompilerParams(vmem_limit_bytes=67043328 - free)


def on_device(
    cache_k,
    cache_v,
    source,
    lengths,
    query,
    new_key,
    new_value,
    resid,
    out_weight,
    norm_gain,
    w_gate,
    w_up,
    w_down,
    expert_ids,
    gate_codes,
):
    groups = lax.axis_size("grp")
    devs = lax.axis_size("dev")
    per, kv_heads, block, head_dim = cache_k.shape
    heads = query.shape[1] // head_dim
    width = query.shape[1]
    hidden = w_gate.shape[1]
    sds = jax.ShapeDtypeStruct
    cache_k, cache_v, source, lengths, out_weight, w_gate, w_up, w_down = (
        pltpu.with_memory_space_constraint(a, pltpu.HBM)
        for a in (cache_k, cache_v, source, lengths, out_weight, w_gate, w_up, w_down)
    )
    plan = sendings(groups)
    sent = pl.pallas_call(
        functools.partial(pack_kernel, groups, per),
        name="pack",
        out_shape=[sds((2, len(ranks), kv_heads, block, head_dim), BF16) for _, ranks in plan],
        in_specs=[HBM, HBM, HBM],
        out_specs=[HBM] * len(plan),
        scratch_shapes=[
            pltpu.SMEM(source.shape, jnp.int32),
            pltpu.VMEM(cache_k.shape, BF16),
            pltpu.VMEM(cache_v.shape, BF16),
            pltpu.SemaphoreType.DMA((3,)),
            pltpu.SemaphoreType.DMA((len(plan), 2, MOVE)),
        ],
        compiler_params=params(56 << 20),
    )(source, cache_k, cache_v)
    moved = [None] * len(plan)
    for at in sorted(range(len(plan)), key=ORDER.index):
        ring = [(g, (g + plan[at][0]) % groups) for g in range(groups)]
        moved[at] = lax.ppermute(sent[at], "grp", ring)

    flat = expert_ids.reshape(-1)
    order = jnp.arange(flat.shape[0], dtype=jnp.int32)
    same = (flat[:, None] == flat[None, :]) & (order[None, :] < order[:, None])
    qflat = flat * CAP + jnp.sum(same.astype(jnp.int32), axis=1)
    qcol = qflat.reshape(per, 2)
    qrow = jnp.concatenate([qcol.T, qcol.T], axis=1)
    codes = gate_codes.astype(F32)
    share = codes / jnp.sum(codes, axis=-1, keepdims=True)
    by_head = query.reshape(per, heads, head_dim).transpose(1, 0, 2)

    row_shape = sds((heads, per, LANES), F32)
    spare_valid, peaks, totals, contexts, start, gains = pl.pallas_call(
        functools.partial(stay_kernel, groups, per),
        name="stay",
        out_shape=(
            sds((per, groups * MOVE * block), F32),
            row_shape,
            row_shape,
            row_shape,
            sds((2, per, LANES), F32),
            sds((2, LANES), F32),
        ),
        in_specs=[HBM] * 4 + [VMEM] + [HBM] * 4 + [VMEM],
        out_specs=(VMEM,) * 6,
        scratch_shapes=[
            pltpu.VMEM(cache_k.shape, BF16),
            pltpu.VMEM(cache_v.shape, BF16),
            pltpu.SMEM(source.shape, jnp.int32),
            pltpu.SMEM(lengths.shape, jnp.int32),
            pltpu.VMEM(new_key.shape, BF16),
            pltpu.VMEM(new_value.shape, BF16),
            pltpu.VMEM(resid.shape, BF16),
            pltpu.VMEM((width // LANES, LANES), BF16),
            pltpu.SemaphoreType.DMA((8,)),
        ],
        compiler_params=params(48 << 20),
        cost_estimate=pl.CostEstimate(flops=0, transcendentals=0, bytes_accessed=16 << 20),
    )(
        source, lengths, cache_k, cache_v, by_head,
        *(
            pltpu.with_memory_space_constraint(a, pltpu.HBM)
            for a in (new_key, new_value, resid, norm_gain.reshape(-1, LANES))
        ),
        qrow,
    )

    ctx = pl.pallas_call(
        arrive_kernel,
        name="arrive",
        out_shape=sds((devs, 2, per, LANES), BF16),
        in_specs=[VMEM] * (5 + len(moved)),
        out_specs=VMEM,
        compiler_params=params(52 << 20),
    )(by_head, spare_valid, peaks, totals, contexts, *moved)
    ctx = lax.all_to_all(ctx, "dev", split_axis=0, concat_axis=0, tiled=True)

    new_k, new_v = pl.pallas_call(
        functools.partial(store_kernel, groups, per),
        name="store",
        out_shape=(sds(cache_k.shape, BF16), sds(cache_v.shape, BF16)),
        in_specs=[HBM] * 4 + [VMEM] * 2 + [pl.BlockSpec(memory_space=pl.ANY)] * len(moved),
        out_specs=(HBM, HBM),
        scratch_shapes=[
            pltpu.VMEM(cache_k.shape, BF16),
            pltpu.VMEM(cache_v.shape, BF16),
            pltpu.SMEM(source.shape, jnp.int32),
            pltpu.SMEM(lengths.shape, jnp.int32),
            pltpu.SemaphoreType.DMA((2,)),
            pltpu.SemaphoreType.DMA((2, per)),
            pltpu.SemaphoreType.DMA((2, per)),
        ],
        compiler_params=params(52 << 20),
        cost_estimate=pl.CostEstimate(flops=0, transcendentals=0, bytes_accessed=8 << 20),
    )(source, lengths, cache_k, cache_v, new_key, new_value, *moved)

    partial_rows = pl.pallas_call(
        project_kernel,
        name="project",
        out_shape=sds((devs, 2, per, LANES), BF16),
        in_specs=[VMEM, HBM],
        out_specs=VMEM,
        scratch_shapes=[
            pltpu.VMEM((8, out_weight.shape[0], width // 8), BF16),
            pltpu.SemaphoreType.DMA((8,)),
        ],
        compiler_params=params(52 << 20),
    )(ctx, out_weight)
    partial_rows = lax.all_to_all(partial_rows, "dev", split_axis=0, concat_axis=0, tiled=True)

    mixed, rows = pl.pallas_call(
        dispatch_kernel,
        name="dispatch",
        out_shape=(
            sds((2, per, LANES), F32),
            sds((groups * devs, 2 * CAP, LANES), BF16),
        ),
        in_specs=[VMEM] * 4,
        out_specs=(VMEM, VMEM),
        compiler_params=params(56 << 20),
    )(partial_rows, start, gains, qrow)
    rows = lax.all_to_all(rows, ("grp", "dev"), split_axis=0, concat_axis=0, tiled=True)

    chunks, down_chunks = 12, 8
    partial_out = pl.pallas_call(
        functools.partial(expert_kernel, groups),
        name="expert",
        out_shape=sds((groups * devs, 2 * CAP, LANES), BF16),
        in_specs=[VMEM, HBM, HBM, HBM],
        out_specs=HBM,
        scratch_shapes=[
            pltpu.VMEM((groups * CAP, width), BF16),
            pltpu.VMEM((groups, devs, 2 * CAP, LANES), BF16),
            pltpu.VMEM((chunks, width // chunks, hidden), BF16),
            pltpu.VMEM((chunks, width // chunks, hidden), BF16),
            pltpu.VMEM((down_chunks, hidden, width // down_chunks), BF16),
            pltpu.SemaphoreType.DMA((3, chunks)),
            pltpu.SemaphoreType.DMA((groups, devs // 2)),
        ],
        compiler_params=params(32 << 20),
    )(rows, w_gate, w_up, w_down)
    partial_out = lax.all_to_all(
        partial_out, ("grp", "dev"), split_axis=0, concat_axis=0, tiled=True
    )

    layer_out = pl.pallas_call(
        final_kernel,
        name="final",
        out_shape=sds(resid.shape, BF16),
        in_specs=[VMEM] * 4,
        out_specs=VMEM,
        compiler_params=params(56 << 20),
    )(partial_out, mixed, qcol, share)
    return (new_k, new_v, layer_out)


def solution(mesh):
    in_specs = (
        P("grp", None, "dev", None),
        P("grp", None, "dev", None),
        P(),
        P("grp"),
        P("grp", None),
        P("grp", None, None),
        P("grp", None, None),
        P("grp", "dev"),
        P("dev", None),
        P(),
        P(None, ("grp", "dev")),
        P(None, ("grp", "dev")),
        P(("grp", "dev"), None),
        P("grp", None),
        P("grp", None),
    )
    out_specs = (P("grp", None, "dev", None), P("grp", None, "dev", None), P("grp", "dev"))
    return jax.shard_map(
        on_device, mesh=mesh, in_specs=in_specs, out_specs=out_specs, check_vma=False
    )
```
